128 devices in a mesh: ctx: 16 (over x, y), head: 8 (over z, core).
Axes of the slice: x: 4, y: 4, z: 4, core: 2. Of those that a mesh axis runs over, the one named last changes fastest.
Arguments:
- queries: bfloat16 [4, 6144, 6144], P(None, 'ctx', 'head'), may hold values from -6 to 6
- keys_values: bfloat16 [4, 6144, 3072], P(None, 'ctx', 'head'), may hold values from -25 to 25
- block_lists: int32 [4, 48, 16], P(None, 'ctx'), may hold values from -1 to 47, as said below
- starts: int32 [4], replicated, may hold values from 0 to 3071, as said below
- norm_gain: bfloat16 [6144], P('head'), may hold values from 0.5 to 1.5
Outputs:
- mixed_out: bfloat16 [4, 6144, 6144], P(None, 'ctx', 'head')
The draws below stay inside these ranges and needn't reach their ends.
Inputs may be any that keep to these rules, and one draw needn't show every extreme that they name: `block_lists`: entry [b, j, s] is a block of 128 positions of prompt b, or -1 for an unused slot. The entries of one list are distinct blocks from the prompt's first block (the block holding starts[b]) up to j, always including that first block and j itself; a list is all -1 where j lies before the first block. For each prompt, the lists of the query blocks held by one index of ctx name at most one block held by any other index of ctx, and this bound is reached. One prompt starts at 0 and one at 3071.
All inputs are finite; a program needn't handle non-finite values.
Results may differ from the reference program's by a relative error of at most 0.0041.
Values may be sent and summed in bfloat16 or wider, within the bound.
A program may use at most 128 MiB of HBM per device.

```python
import math
import jax
import jax.numpy as jnp
from jax import lax

HD = 96
NSEQ = 4
BLK = 128
TOPK = 16
HEADS = 64
KV_HEADS = 16
GROUP = 4
QBS = 3
SEQ_LEN = 6144
NBLK = 48


def starts_and_lists(key):
    base_key = jax.random.fold_in(key, 11)
    key_inner, key_shuffle, key_picks, key_rank = jax.random.split(base_key, 4)
    half_len = SEQ_LEN // 2
    inner_starts = jax.random.randint(key_inner, (NSEQ - 2,), 1, half_len - 1).astype(jnp.int32)
    base_starts = jnp.concatenate([jnp.array([0, half_len - 1], jnp.int32), inner_starts])
    shuffle = jax.random.permutation(key_shuffle, NSEQ)
    seq_starts = base_starts[shuffle]
    first_block = seq_starts // BLK
    owner_count = NBLK // QBS
    owner_ids = jnp.arange(owner_count, dtype=jnp.int32)
    lowest = jnp.maximum(first_block[:, None], owner_ids[None, :] * QBS)
    span_len = (owner_ids[None, :] + 1) * QBS - lowest
    offsets = jax.random.randint(key_picks, (NSEQ, owner_count, owner_count), 0, 1 << 20) % jnp.maximum(span_len[:, None, :], 1)
    picks = jnp.where(span_len[:, None, :] > 0, lowest[:, None, :] + offsets, -1)
    picks = jnp.where(owner_ids[None, None, :] == (first_block // QBS)[:, None, None], first_block[:, None, None], picks)
    blocks = jnp.arange(NBLK, dtype=jnp.int32)
    block_owner = blocks // QBS
    pick_table = picks[:, block_owner[:, None], block_owner[None, :]]
    from_picks = (block_owner[None, None, :] < block_owner[None, :, None]) & (pick_table == blocks[None, None, :])
    on_device = (block_owner[None, None, :] == block_owner[None, :, None]) & (blocks[None, None, :] <= blocks[None, :, None]) & (blocks[None, None, :] >= first_block[:, None, None])
    usable = (from_picks | on_device) & (blocks[None, :, None] >= first_block[:, None, None])
    forced = (blocks[None, None, :] == first_block[:, None, None]) | (blocks[None, None, :] == blocks[None, :, None])
    random_rank = jax.random.randint(key_rank, (NSEQ, NBLK, NBLK), 0, 1 << 20) * NBLK + blocks[None, None, :]
    ranking = jnp.where(forced, (1 << 29) + blocks[None, None, :], random_rank)
    ranking = jnp.where(usable, ranking, -1)
    top_values, top_index = lax.top_k(ranking, TOPK)
    block_ids = jnp.where(top_values >= 0, top_index, -1).astype(jnp.int32)
    return (seq_starts, block_ids)


def draw_starts(key, part):
    return starts_and_lists(key)[0]


def draw_block_lists(key, part):
    return starts_and_lists(key)[1]


def draw_queries(key, part):
    noise_key = jax.random.fold_in(key, 5)
    values = jnp.clip(jax.random.normal(noise_key, (NSEQ, SEQ_LEN, HEADS * HD), jnp.float32), -5.0, 5.0)
    return values.astype(jnp.bfloat16)


def draw_keys_values(key, part):
    noise_key = jax.random.fold_in(key, 6)
    value_key = jax.random.fold_in(key, 7)
    head_scale = 3.0 ** (jnp.arange(KV_HEADS, dtype=jnp.float32) / max(KV_HEADS - 1, 1))
    full_shape = (NSEQ, SEQ_LEN, KV_HEADS, HD)
    key_part = jnp.clip(jax.random.normal(noise_key, full_shape, jnp.float32), -5.0, 5.0)
    value_part = jnp.clip(jax.random.normal(value_key, full_shape, jnp.float32), -5.0, 5.0) * head_scale[None, None, :, None]
    stacked = jnp.stack([key_part, value_part], axis=3).reshape(NSEQ, SEQ_LEN, KV_HEADS * 2 * HD)
    return stacked.astype(jnp.bfloat16)


def setup_inputs(seed: int = 0) -> dict:
    key_of = jax.random.split(jax.random.key(seed), 6)
    queries = draw_queries(jax.random.fold_in(key_of[5], 71), 0)
    keys_values = draw_keys_values(jax.random.fold_in(key_of[5], 71), 0)
    block_lists = draw_block_lists(jax.random.fold_in(key_of[5], 71), 0)
    starts = draw_starts(jax.random.fold_in(key_of[5], 71), 0)
    norm_gain = jnp.clip(1.0 + 0.1 * jax.random.normal(key_of[4], (HEADS * HD,), jnp.float32), 0.5, 1.5).astype(jnp.bfloat16)
    return {"queries": queries, "keys_values": keys_values, "block_lists": block_lists, "starts": starts, "norm_gain": norm_gain}


epsilon = 1e-06
masked_score = -1e+30

def feature_map(values):
    return jax.nn.elu(values) + 1.0

def linear_branch(queries, keys_values, starts):
    query_stretches = queries.reshape(NSEQ, NBLK, BLK, KV_HEADS, GROUP, HD)
    kv_stretches = keys_values.reshape(NSEQ, NBLK, BLK, KV_HEADS, 2, HD)
    positions = jnp.arange(SEQ_LEN, dtype=jnp.int32).reshape(NBLK, BLK)
    usable = positions[None] >= starts[:, None, None]
    phi_query = lax.optimization_barrier(feature_map(query_stretches.astype(jnp.float32)).astype(jnp.bfloat16))
    phi_key = lax.optimization_barrier((feature_map(kv_stretches[:, :, :, :, 0, :].astype(jnp.float32)) * usable[:, :, :, None, None]).astype(jnp.bfloat16))
    value_stretches = kv_stretches[:, :, :, :, 1, :]
    causal = jnp.arange(BLK)[:, None] >= jnp.arange(BLK)[None, :]
    highest = lax.Precision.HIGHEST

    def advance(carry, inputs):
        state, normal = carry
        query_part, key_part, value_part, row_usable = inputs
        query_float = query_part.astype(jnp.float32)
        key_float = key_part.astype(jnp.float32)
        value_float = value_part.astype(jnp.float32)
        inner_scores = jnp.einsum('btgxd,bsgd->bgxts', query_float, key_float, precision=highest)
        inner_scores = jnp.where(causal, inner_scores, 0.0)
        inner_sum = jnp.transpose(lax.optimization_barrier(jnp.sum(inner_scores, axis=-1)), (0, 3, 1, 2))
        rounded = lax.optimization_barrier(inner_scores.astype(jnp.bfloat16)).astype(jnp.float32)
        inner_num = jnp.einsum('bgxts,bsge->btgxe', rounded, value_float, precision=highest)
        state_num = jnp.einsum('btgxd,bgde->btgxe', query_float, state, precision=highest)
        state_den = jnp.einsum('btgxd,bgd->btgx', query_float, normal, precision=highest)
        row_ok = row_usable[:, :, None, None]
        denominator = jnp.where(row_ok, inner_sum + state_den, 1.0)
        result = jnp.where(row_ok[..., None], (inner_num + state_num) / denominator[..., None], 0.0)
        state = state + jnp.einsum('bsgd,bsge->bgde', key_float, value_float, precision=highest)
        normal = normal + lax.optimization_barrier(jnp.sum(key_float, axis=1))
        return ((state, normal), result)
    initial = (jnp.zeros((NSEQ, KV_HEADS, HD, HD), jnp.float32), jnp.zeros((NSEQ, KV_HEADS, HD), jnp.float32))
    inputs = (jnp.moveaxis(phi_query, 1, 0), jnp.moveaxis(phi_key, 1, 0), jnp.moveaxis(value_stretches, 1, 0), jnp.moveaxis(usable, 1, 0))
    unused, outputs = lax.scan(advance, initial, inputs)
    return jnp.moveaxis(outputs, 0, 1).reshape(NSEQ, SEQ_LEN, HEADS * HD)

def sparse_branch(queries, keys_values, block_lists, starts):
    query_blocks = queries.reshape(NSEQ * NBLK, BLK, KV_HEADS, GROUP, HD)
    kv_blocks = keys_values.reshape(NSEQ, NBLK, BLK, KV_HEADS, 2, HD)
    flat_lists = block_lists.reshape(NSEQ * NBLK, TOPK)
    score_scale = 1.0 / math.sqrt(HD)
    offsets = jnp.arange(BLK, dtype=jnp.int32)

    def one_block(entry):
        seq_index = entry // NBLK
        block_index = entry % NBLK
        query_block = lax.dynamic_index_in_dim(query_blocks, entry, 0, False).astype(jnp.float32)
        chosen = lax.dynamic_index_in_dim(flat_lists, entry, 0, False)
        safe_ids = jnp.maximum(chosen, 0)
        seq_blocks = lax.dynamic_index_in_dim(kv_blocks, seq_index, 0, False)
        picked = jnp.take(seq_blocks, safe_ids, axis=0).reshape(TOPK * BLK, KV_HEADS, 2, HD)
        key_float = picked[:, :, 0, :].astype(jnp.float32)
        value_float = picked[:, :, 1, :].astype(jnp.float32)
        key_pos = (safe_ids[:, None] * BLK + offsets[None, :]).reshape(TOPK * BLK)
        listed = jnp.repeat(chosen >= 0, BLK)
        query_pos = block_index * BLK + offsets
        first_live = lax.dynamic_index_in_dim(starts, seq_index, 0, False)
        allowed = listed[None, :] & (key_pos[None, :] <= query_pos[:, None]) & (key_pos[None, :] >= first_live)
        scores = jnp.einsum('xghd,kgd->ghxk', query_block, key_float) * score_scale
        scores = jnp.where(allowed[None, None], scores, masked_score)
        top_score = lax.optimization_barrier(jnp.max(scores, axis=-1, keepdims=True))
        weights = jnp.where(allowed[None, None], jnp.exp(scores - top_score), 0.0)
        weight_sum = jnp.transpose(lax.optimization_barrier(jnp.sum(weights, axis=-1)), (2, 0, 1))
        rounded = lax.optimization_barrier(weights.astype(jnp.bfloat16)).astype(jnp.float32)
        gathered = jnp.einsum('ghxk,kge->xghe', rounded, value_float)
        row_ok = (query_pos >= first_live)[:, None, None]
        return jnp.where(row_ok[..., None], gathered / jnp.where(row_ok, weight_sum, 1.0)[..., None], 0.0)
    outputs = lax.map(one_block, jnp.arange(NSEQ * NBLK, dtype=jnp.int32))
    return outputs.reshape(NSEQ, SEQ_LEN, HEADS * HD)

def reference(queries, keys_values, block_lists, starts, norm_gain):
    linear = linear_branch(queries, keys_values, starts)
    sparse = sparse_branch(queries, keys_values, block_lists, starts)
    combined = linear + sparse
    mean_square = lax.optimization_barrier(jnp.mean(combined * combined, axis=-1, keepdims=True))
    scaled = combined * lax.rsqrt(mean_square + epsilon) * norm_gain.astype(jnp.float32)
    return scaled.astype(jnp.bfloat16)
```

```python
import math

import jax
import jax.numpy as jnp
from jax import lax
from jax.experimental import pallas as pl
from jax.experimental.pallas import tpu as pltpu
from jax.sharding import PartitionSpec as P

HD = 96
BLK = 128
TOPK = 16
QBS = 3
NCTX = 16
GROUP = 4
LANES = 128
OWN = QBS
SLOTS = 20
epsilon = 1e-06
NEG = -1e30
SCALE = math.log2(math.e) / math.sqrt(HD)
NT = (((1,), (1,)), ((), ()))
TN = (((0,), (0,)), ((), ()))
NN = (((1,), (0,)), ((), ()))


def dot(a, b, dims):
    return lax.dot_general(a, b, dims, preferred_element_type=jnp.float32)


def feature(x):
    x = x.astype(jnp.float32)
    return jnp.where(x > 0, x + 1.0, jnp.exp(jnp.minimum(x, 0.0)))


def place(block, bias, kx, vx, slot):
    rows = pl.ds(pl.multiple_of(slot * BLK, BLK), BLK)
    ones = jnp.ones((BLK, LANES - HD), jnp.bfloat16)
    for g in range(2):
        k = block[:, 2 * g * HD : (2 * g + 1) * HD]
        v = block[:, (2 * g + 1) * HD : (2 * g + 2) * HD]
        kx[g, rows, :] = jnp.concatenate([k, bias], axis=1)
        vx[g, rows, :] = jnp.concatenate([v, ones], axis=1)


def kernel(
    starts, picks, q_ref, kv_ref, recv_ref, bias_ref, prior_ref, out_ref, kx, vx, qx, fq, fk, sc, mx
):
    b = pl.program_id(0)
    me = lax.axis_index("ctx")
    start = starts[b]
    tail = LANES - HD
    lane = lax.broadcasted_iota(jnp.int32, (BLK, tail), 1)
    row = lax.broadcasted_iota(jnp.int32, (BLK, tail), 0)
    wide_lane = lax.broadcasted_iota(jnp.int32, (BLK, LANES), 1)
    wide_row = lax.broadcasted_iota(jnp.int32, (BLK, LANES), 0)

    @pl.when(b == 0)
    def _():
        for g in range(2):
            kx[g] = jnp.full((SLOTS * BLK, LANES), NEG, jnp.bfloat16)
            kx[g, :, 0:HD] = jnp.zeros((SLOTS * BLK, HD), jnp.bfloat16)
            vx[g] = jnp.zeros((SLOTS * BLK, LANES), jnp.bfloat16)

    def tail_bias(slot_row, first_pos):
        listed = bias_ref[0, pl.ds(slot_row, 1), HD:LANES]
        late = jnp.where((lane == QBS) & (row + first_pos < start), NEG, 0.0)
        return (listed + late).astype(jnp.bfloat16)

    for k in range(QBS):
        pos = (me * QBS + k) * BLK
        block = kv_ref[0, k * BLK : (k + 1) * BLK, :]
        place(block, tail_bias(NCTX + k, pos), kx, vx, k)
        for g in range(2):
            f = feature(block[:, 2 * g * HD : (2 * g + 1) * HD])
            live = lax.broadcasted_iota(jnp.int32, (BLK, HD), 0) + pos >= start
            f = jnp.where(live, f, 0.0).astype(jnp.bfloat16)
            fk[g, k * BLK : (k + 1) * BLK, :] = jnp.concatenate(
                [f, jnp.zeros((BLK, tail), jnp.bfloat16)], axis=1
            )

    def bring(s, carry):
        pos = (s * QBS + picks[b, s]) * BLK
        place(recv_ref[0, s], tail_bias(s, pos), kx, vx, OWN + s)
        return carry

    lax.fori_loop(0, me, bring, 0)

    for qb in range(QBS):
        marks = jnp.where((lane == qb) | (lane == QBS), 1.0, 0.0).astype(jnp.bfloat16)
        for h in range(2 * GROUP):
            g, x = h // GROUP, h % GROUP
            piece = q_ref[0, qb * BLK : (qb + 1) * BLK, h * HD : (h + 1) * HD]
            base = (qb * 2 + g) * GROUP * BLK + x * BLK
            qx[base : base + BLK, :] = jnp.concatenate([piece, marks], axis=1)
            fq[base : base + BLK, :] = jnp.concatenate(
                [feature(piece).astype(jnp.bfloat16), jnp.zeros((BLK, tail), jnp.bfloat16)], axis=1
            )

    causal = wide_row >= wide_lane
    rows = GROUP * BLK
    causal4 = jnp.concatenate([causal] * GROUP, axis=0)
    chunks = (me + OWN + 1) // 2
    for g in range(2):
        state = prior_ref[0, g]
        for qb in range(QBS):
            base = (qb * 2 + g) * rows
            q = qx[base : base + rows, :]
            diag = dot(q, kx[g, qb * BLK : (qb + 1) * BLK, :], NT)
            diag = jnp.where(causal4, diag, NEG)
            sc[:, qb * BLK : (qb + 1) * BLK] = diag
            top = diag
            for k in range(QBS):
                if k < qb:
                    s = dot(q, kx[g, k * BLK : (k + 1) * BLK, :], NT)
                    top = jnp.maximum(top, s)
                    sc[:, k * BLK : (k + 1) * BLK] = s
                elif k > qb:
                    sc[:, k * BLK : (k + 1) * BLK] = jnp.full((rows, BLK), NEG, jnp.float32)
            s = dot(q, kx[g, OWN * BLK : (OWN + 1) * BLK, :], NT)
            sc[:, OWN * BLK : (OWN + 1) * BLK] = s
            mx[...] = jnp.maximum(top, s)

            def score(c, carry):
                at = pl.ds(pl.multiple_of(c * 2 * BLK, 2 * BLK), 2 * BLK)
                s = dot(q, kx[g, at, :], NT)
                sc[:, at] = s
                mx[...] = jnp.maximum(mx[...], jnp.maximum(s[:, :BLK], s[:, BLK:]))
                return carry

            lax.fori_loop(2, chunks, score, 0)
            peak = jnp.max(mx[...], axis=1, keepdims=True)

            def weigh(c, acc):
                at = pl.ds(pl.multiple_of(c * 2 * BLK, 2 * BLK), 2 * BLK)
                w = jnp.exp2((sc[:, at] - peak) * SCALE).astype(jnp.bfloat16)
                return acc + dot(w, vx[g, at, :], NN)

            acc = lax.fori_loop(0, chunks, weigh, jnp.zeros((rows, LANES), jnp.float32))
            fqv = fq[base : base + rows, :]
            fkv = fk[g, qb * BLK : (qb + 1) * BLK, :]
            vown = vx[g, qb * BLK : (qb + 1) * BLK, :]
            inner = jnp.where(causal4, dot(fqv, fkv, NT), 0.0).astype(jnp.bfloat16)
            high = state.astype(jnp.bfloat16)
            low = (state - high.astype(jnp.float32)).astype(jnp.bfloat16)
            lin = dot(inner, vown, NN) + dot(fqv, high, NN) + dot(fqv, low, NN)
            if qb < QBS - 1:
                state = state + dot(fkv, vown, TN)
            live = lax.broadcasted_iota(jnp.int32, (BLK, 1), 0) + (me * QBS + qb) * BLK >= start
            live4 = jnp.concatenate([live] * GROUP, axis=0)
            den = jnp.where(live4, lin[:, HD : HD + 1], 1.0)
            both = lin * (1.0 / den) + acc * (1.0 / acc[:, HD : HD + 1])
            both = jnp.where(live4, both, 0.0)
            out_ref[0, qb * BLK : (qb + 1) * BLK, g * GROUP * HD : (g + 1) * GROUP * HD] = (
                jnp.concatenate(
                    [both[x * BLK : (x + 1) * BLK, :HD] for x in range(GROUP)], axis=1
                )
            )


def on_device(queries, keys_values, block_lists, starts, norm_gain):
    nseq, length, width = queries.shape
    kv_width = keys_values.shape[2]
    me = lax.axis_index("ctx")
    ctx = jnp.arange(NCTX, dtype=jnp.int32)
    owner = jnp.where(block_lists >= 0, block_lists // QBS, -1)
    hit = owner[..., None] == ctx
    picks = jnp.max(jnp.where(hit, (block_lists % QBS)[..., None], 0), axis=(1, 2))
    listed = jnp.any(hit, axis=2)
    own = jnp.any(
        block_lists[..., None] == me * QBS + jnp.arange(QBS, dtype=jnp.int32), axis=2
    )
    flags = jnp.concatenate([listed, own, jnp.zeros_like(own)[..., :2]], axis=2)
    flags = jnp.where(flags, 0.0, NEG)
    bias = jnp.pad(
        jnp.transpose(flags, (0, 2, 1)), ((0, 0), (0, 0), (HD, LANES - HD - QBS))
    )
    wanted = lax.dynamic_index_in_dim(lax.all_gather(picks, "ctx", axis=0), me, 2, False)
    blocks = keys_values.reshape(nseq, QBS, BLK, kv_width)
    sent = jnp.stack(
        [
            jnp.where(
                (wanted[:, b] == 0)[:, None, None],
                blocks[b, 0],
                jnp.where((wanted[:, b] == 1)[:, None, None], blocks[b, 1], blocks[b, 2]),
            )
            for b in range(nseq)
        ]
    )
    recv = lax.all_to_all(sent, "ctx", 1, 1, tiled=True)

    positions = me * length + jnp.arange(length, dtype=jnp.int32)
    usable = positions[None, :] >= starts[:, None]
    pairs = keys_values.reshape(nseq, length, 2, 2, HD)
    phi = (feature(pairs[:, :, :, 0]) * usable[:, :, None, None]).astype(jnp.bfloat16)
    vals = jnp.concatenate(
        [pairs[:, :, :, 1], jnp.ones((nseq, length, 2, LANES - HD), jnp.bfloat16)], axis=3
    )
    state = jnp.einsum("btgd,btge->bgde", phi, vals, preferred_element_type=jnp.float32)
    every = lax.all_gather(state.astype(jnp.bfloat16), "ctx")
    prior = jnp.sum(
        jnp.where((ctx < me)[:, None, None, None, None], every.astype(jnp.float32), 0.0), axis=0
    )
    prior = jnp.pad(prior, ((0, 0), (0, 0), (0, LANES - HD), (0, 0)))

    smem = pl.BlockSpec(memory_space=pltpu.SMEM)
    combined = pl.pallas_call(
        kernel,
        grid=(nseq,),
        in_specs=[
            smem,
            smem,
            pl.BlockSpec((1, length, width), lambda b: (b, 0, 0)),
            pl.BlockSpec((1, length, kv_width), lambda b: (b, 0, 0)),
            pl.BlockSpec((1, NCTX, BLK, kv_width), lambda b: (b, 0, 0, 0)),
            pl.BlockSpec((1, NCTX + QBS + 2, LANES), lambda b: (b, 0, 0)),
            pl.BlockSpec((1, 2, LANES, LANES), lambda b: (b, 0, 0, 0)),
        ],
        out_specs=pl.BlockSpec((1, length, width), lambda b: (b, 0, 0)),
        out_shape=jax.ShapeDtypeStruct((nseq, length, width), jnp.float32),
        scratch_shapes=[
            pltpu.VMEM((2, SLOTS * BLK, LANES), jnp.bfloat16),
            pltpu.VMEM((2, SLOTS * BLK, LANES), jnp.bfloat16),
            pltpu.VMEM((QBS * 2 * GROUP * BLK, LANES), jnp.bfloat16),
            pltpu.VMEM((QBS * 2 * GROUP * BLK, LANES), jnp.bfloat16),
            pltpu.VMEM((2, QBS * BLK, LANES), jnp.bfloat16),
            pltpu.VMEM((GROUP * BLK, SLOTS * BLK), jnp.float32),
            pltpu.VMEM((GROUP * BLK, LANES), jnp.float32),
        ],
        compiler_params=pltpu.CompilerParams(vmem_limit_bytes=48 << 20),
    )(starts, picks, queries, keys_values, recv, bias, prior)

    squares = jnp.sum(combined * combined, axis=-1)
    all_squares = lax.psum(squares, "head")
    full_width = width * lax.axis_size("head")
    scaled = (
        combined
        * lax.rsqrt(all_squares / full_width + epsilon)[..., None]
        * norm_gain.astype(jnp.float32)
    )
    return scaled.astype(jnp.bfloat16)


def solution(mesh):
    return jax.shard_map(
        on_device,
        mesh=mesh,
        in_specs=(
            P(None, "ctx", "head"),
            P(None, "ctx", "head"),
            P(None, "ctx", None),
            P(),
            P("head"),
        ),
        out_specs=P(None, "ctx", "head"),
        check_vma=False,
    )
```

```python
import math

import jax
import jax.numpy as jnp
from jax import lax
from jax.experimental import pallas as pl
from jax.experimental.pallas import tpu as pltpu
from jax.sharding import PartitionSpec as P

HD = 96
BLK = 128
QBS = 3
NSEQ = 4
SIDE = 4
NCTX = 16
NHEAD = 8
GROUP = 4
LANES = 128
LEN = QBS * BLK
KVW = 4 * HD
WIDTH = 2 * GROUP * HD
ROWS = GROUP * BLK
OWN0 = NCTX - 1
SLOTS = OWN0 + QBS
NCH = SLOTS // 2
TAIL = LANES - HD
epsilon = 1e-06
NEG = -1e30
SCALE = math.log2(math.e) / math.sqrt(HD)
NT = (((1,), (1,)), ((), ()))
TN = (((0,), (0,)), ((), ()))
NN = (((1,), (0,)), ((), ()))
BF = jnp.bfloat16
F32 = jnp.float32
MESH = pl.DeviceIdType.MESH


def dot(a, b, dims):
    return lax.dot_general(a, b, dims, preferred_element_type=F32)


def feature(x):
    x = x.astype(F32)
    return jnp.where(x > 0, x + 1.0, jnp.exp(jnp.minimum(x, 0.0)))


def kernel(
    starts, picks, q_hbm, kv, bias_ref, pickrows, gain, out_ref,
    q_ref, near, packed, far, relay, pk_in, st_own, st_y, st_row, st_x,
    prior, fk, vown, lin_ref, comb, kx, vx, qx, fq, sc, pw, mx, sq, sq_in,
    q_sem, s_send, s_recv, p_send, p_recv, t_send, t_recv, h_send, h_recv,
):
    me = lax.axis_index("ctx")
    hd = lax.axis_index("head")
    x, y = me // SIDE, me % SIDE

    def device(o, du, dv):
        dx, dy = (du, dv) if o == 0 else (dv, du)
        return ((x + dx + 2 * SIDE) % SIDE) * SIDE + (y + dy + 2 * SIDE) % SIDE

    def copy(src, dst, send, recv, target):
        return pltpu.make_async_remote_copy(
            src_ref=src, dst_ref=dst, send_sem=send, recv_sem=recv,
            device_id={"ctx": target}, device_id_type=MESH,
        )

    q_copy = pltpu.make_async_copy(q_hbm, q_ref, q_sem)
    q_copy.start()
    barrier = pltpu.get_barrier_semaphore()
    for o in range(2):
        for d in range(1, SIDE):
            pl.semaphore_signal(
                barrier, inc=1, device_id={"ctx": device(o, d, 0)}, device_id_type=MESH
            )
    for d in range(1, NHEAD):
        pl.semaphore_signal(
            barrier, inc=1, device_id={"head": (hd + d) % NHEAD}, device_id_type=MESH
        )
    pl.semaphore_wait(barrier, 2 * (SIDE - 1) + NHEAD - 1)

    def pick_copy(o, d):
        i = o * 3 + d - 1
        return copy(pickrows, pk_in.at[o, d - 1], p_send.at[i], p_recv.at[i], device(o, 0, -d))

    def hop(b, i):
        o = b % 2
        half = LEN // 2
        src, dst, du, dv = [
            (kv.at[b], near.at[b, 0], 1, 0),
            (kv.at[b], near.at[b, 2], -1, 0),
            (near.at[b, 0, 0:half], near.at[b, 1, 0:half], 1, 0),
            (near.at[b, 2, half:LEN], near.at[b, 1, half:LEN], -1, 0),
            (packed.at[b, 0], far.at[b, 0], 0, 1),
            (packed.at[b, 2], far.at[b, 2], 0, -1),
            (packed.at[b, 1, 0:2], relay.at[b, 0], 0, 1),
            (packed.at[b, 1, 2:4], relay.at[b, 1], 0, -1),
            (relay.at[b, 0], far.at[b, 1, 0:2], 0, 1),
            (relay.at[b, 1], far.at[b, 1, 2:4], 0, -1),
        ][i]
        return copy(src, dst, s_send.at[b, i], s_recv.at[b, i], device(o, du, dv))

    def start(b, *which):
        for i in which:
            hop(b, i).start()

    def arrived(b, *which):
        for i in which:
            hop(b, i).wait_recv()

    for b in (0, 1):
        start(b, 0, 1)
    for o in range(2):
        for d in range(1, SIDE):
            pick_copy(o, d).start()

    row96 = lax.broadcasted_iota(jnp.int32, (BLK, HD), 0)
    lane = lax.broadcasted_iota(jnp.int32, (BLK, TAIL), 1)
    row = lax.broadcasted_iota(jnp.int32, (BLK, TAIL), 0)
    zeros = jnp.zeros((BLK, TAIL), BF)
    ones = jnp.ones((BLK, TAIL), BF)

    def summary(b, carry):
        first = starts[b]
        for k in range(QBS):
            at = slice(k * BLK, (k + 1) * BLK)
            live = row96 + (me * QBS + k) * BLK >= first
            for g in range(2):
                key = kv[b, at, 2 * g * HD : (2 * g + 1) * HD]
                f = jnp.where(live, feature(key), 0.0).astype(BF)
                fk[b, g, at, :] = jnp.concatenate([f, zeros], axis=1)
                v = kv[b, at, (2 * g + 1) * HD : (2 * g + 2) * HD]
                vown[b, g, at, :] = jnp.concatenate([v, ones], axis=1)
        for g in range(2):
            t = dot(fk[b, g], vown[b, g], TN)
            st_own[b, g] = t[:HD].astype(BF)
        return carry

    lax.fori_loop(0, NSEQ, summary, 0)

    def state_copy(o, d):
        i = (1 - o) * 3 + d - 1
        src, dst = (st_row, st_x) if o == 0 else (st_own, st_y)
        return copy(src, dst.at[d - 1], t_send.at[i], t_recv.at[i], device(o, d, 0))

    for d in range(1, SIDE):
        state_copy(1, d).start()
    for b in (0, 1):
        arrived(b, 0, 1)
        start(b, 2, 3)
    for d in range(1, SIDE):
        state_copy(1, d).wait_recv()

    def rows_sum(b, carry):
        for g in range(2):
            total = st_own[b, g].astype(F32)
            before = jnp.zeros((HD, LANES), F32)
            for d in range(1, SIDE):
                part = st_y[d - 1, b, g].astype(F32)
                total = total + part
                before = before + jnp.where(y >= d, part, 0.0)
            st_row[b, g] = total.astype(BF)
            prior[b, g] = before
        return carry

    lax.fori_loop(0, NSEQ, rows_sum, 0)
    for d in range(1, SIDE):
        state_copy(0, d).start()
    for o in range(2):
        for d in range(1, SIDE):
            pick_copy(o, d).wait_recv()

    def source(o, du, dv):
        return device(o, -du, -dv)

    def choose(table, at, blocks, put):
        w = jnp.broadcast_to(table[pl.ds(at, 1), :], (BLK, LANES)).astype(BF)
        m0, m1 = w == 0.0, w == 1.0
        for c in range(KVW // LANES):
            cols = slice(c * LANES, (c + 1) * LANES)
            b0, b1, b2 = [blocks[k * BLK : (k + 1) * BLK, cols] for k in range(QBS)]
            put(cols, jnp.where(m0, b0, jnp.where(m1, b1, b2)))

    def pack(b):
        o = b % 2
        for dv in range(1, SIDE):
            for du in range(SIDE):
                blocks = kv.at[b] if du == 0 else near.at[b, du - 1]

                def put(cols, val, dv=dv, du=du):
                    packed[b, dv - 1, du, :, cols] = val

                choose(pk_in.at[o, dv - 1], b * NCTX + source(o, du, 0), blocks, put)

    for b in (0, 1):
        arrived(b, 2, 3)
        pack(b)
        start(b, 4, 5, 6, 7)
    for b in (2, 3):
        start(b, 0, 1)

    for d in range(1, SIDE):
        state_copy(0, d).wait_recv()

    def add_x(b, carry):
        for g in range(2):
            before = prior[b, g]
            for d in range(1, SIDE):
                before = before + jnp.where(x >= d, st_x[d - 1, b, g].astype(F32), 0.0)
            prior[b, g] = before
        return carry

    lax.fori_loop(0, NSEQ, add_x, 0)
    q_copy.wait()

    trow = lax.broadcasted_iota(jnp.int32, (ROWS, BLK), 0) % BLK
    tlane = lax.broadcasted_iota(jnp.int32, (ROWS, BLK), 1)
    causal = trow >= tlane

    def live_rows(b, qb):
        r = lax.broadcasted_iota(jnp.int32, (ROWS, 1), 0) % BLK
        return r + (me * QBS + qb) * BLK >= starts[b]

    def linear(b, carry):
        for g in range(2):
            state = jnp.concatenate([prior[b, g], jnp.zeros((TAIL, LANES), F32)], axis=0)
            for qb in range(QBS):
                for h in range(GROUP):
                    c = (g * GROUP + h) * HD
                    piece = q_ref[b, qb * BLK : (qb + 1) * BLK, c : c + HD]
                    fq[qb % 2, h * BLK : (h + 1) * BLK, :] = jnp.concatenate(
                        [feature(piece).astype(BF), zeros], axis=1
                    )
                fqv = fq[qb % 2]
                fkv = fk[b, g, qb * BLK : (qb + 1) * BLK, :]
                vo = vown[b, g, qb * BLK : (qb + 1) * BLK, :]
                inner = jnp.where(causal, dot(fqv, fkv, NT), 0.0).astype(BF)
                high = state.astype(BF)
                low = (state - high.astype(F32)).astype(BF)
                lin = dot(inner, vo, NN) + dot(fqv, high, NN) + dot(fqv, low, NN)
                if qb < QBS - 1:
                    state = state + dot(fkv, vo, TN)
                den = jnp.where(live_rows(b, qb), lin[:, HD : HD + 1], 1.0)
                lin_ref[b, g * QBS + qb] = lin * (1.0 / den)
        return carry

    lax.fori_loop(0, 2, linear, 0)
    for b in (0, 1):
        arrived(b, 6, 7)
        start(b, 8, 9)
    for b in (2, 3):
        arrived(b, 0, 1)
        start(b, 2, 3)
    lax.fori_loop(2, NSEQ, linear, 0)
    for b in (2, 3):
        arrived(b, 2, 3)
        pack(b)
        start(b, 4, 5, 6, 7)

    def place(slot, load, bias):
        at = slice(slot * BLK, (slot + 1) * BLK)
        for g in range(2):
            k = load(2 * g * HD, (2 * g + 1) * HD)
            v = load((2 * g + 1) * HD, (2 * g + 2) * HD)
            kx[g, at, :] = jnp.concatenate([k, bias], axis=1)
            vx[g, at, :] = jnp.concatenate([v, ones], axis=1)

    def tail_bias(b, slot_row, pos):
        listed = bias_ref[b, pl.ds(slot_row, 1), HD:LANES]
        late = jnp.where((lane == QBS) & (row + pos < starts[b]), NEG, 0.0)
        return (listed + late).astype(BF)

    def scores(i):
        g, qb = i // QBS, i % QBS
        q = qx[i * ROWS : (i + 1) * ROWS, :]
        top = None
        for c in range(NCH):
            at = slice(c * 2 * BLK, (c + 1) * 2 * BLK)
            s = dot(q, kx[g, at, :], NT)
            parts = []
            for n in range(2):
                k = 2 * c + n - OWN0
                part = s[:, n * BLK : (n + 1) * BLK]
                if k == qb:
                    part = jnp.where(causal, part, NEG)
                parts.append(part)
                sc[i % 2, :, (2 * c + n) * BLK : (2 * c + n + 1) * BLK] = part
            t = jnp.maximum(parts[0], parts[1])
            top = t if top is None else jnp.maximum(top, t)
        mx[i % 2] = top

    def weigh(b, i):
        g, qb = i // QBS, i % QBS
        peak = jnp.max(mx[i % 2], axis=1, keepdims=True)
        for c in range(NCH):
            at = slice(c * 2 * BLK, (c + 1) * 2 * BLK)
            pw[i % 2, :, at] = jnp.exp2((sc[i % 2, :, at] - peak) * SCALE).astype(BF)
        acc = dot(pw[i % 2], vx[g], NN)
        both = lin_ref[b, i] + acc * (1.0 / acc[:, HD : HD + 1])
        both = jnp.where(live_rows(b, qb), both, 0.0)
        comb[b, qb * BLK : (qb + 1) * BLK, g * GROUP * HD : (g + 1) * GROUP * HD] = (
            jnp.concatenate([both[h * BLK : (h + 1) * BLK, :HD] for h in range(GROUP)], axis=1)
        )

    def attend(b, carry):
        o = b % 2
        u_x = 1 - o

        for which in range(2):

            @pl.when(b == 2)
            def _(which=which):
                arrived(2 + which, 6, 7)
                start(2 + which, 8, 9)

        for which in range(NSEQ):

            @pl.when(b == which)
            def _(which=which):
                arrived(which, 4, 5, 8, 9)

        def source_of(du, dv):
            sx = (x + 8 - du * u_x - dv * o) % SIDE
            sy = (y + 8 - dv * u_x - du * o) % SIDE
            return sx * SIDE + sy

        slot = 0
        for dv in range(SIDE):
            for du in range(SIDE):
                if du == 0 and dv == 0:
                    continue
                s = source_of(du, dv)
                pos = (s * QBS + picks[b, s]) * BLK
                tb = tail_bias(b, s, pos)
                if dv == 0:
                    got = []
                    choose(
                        pickrows, b * NCTX + s, near.at[b, du - 1],
                        lambda cols, val, got=got: got.append(val),
                    )
                    whole = jnp.concatenate(got, axis=1)
                    place(slot, lambda l, r, w=whole: w[:, l:r], tb)
                else:
                    place(slot, lambda l, r, dv=dv, du=du: far[b, dv - 1, du, :, l:r], tb)
                slot += 1
        for k in range(QBS):
            tb = tail_bias(b, NCTX + k, (me * QBS + k) * BLK)
            place(slot, lambda l, r, k=k: kv[b, k * BLK : (k + 1) * BLK, l:r], tb)
            slot += 1
        for qb in range(QBS):
            marks = jnp.where((lane == qb) | (lane == QBS), 1.0, 0.0).astype(BF)
            for h in range(2 * GROUP):
                g, r = h // GROUP, h % GROUP
                piece = q_ref[b, qb * BLK : (qb + 1) * BLK, h * HD : (h + 1) * HD]
                base = (g * QBS + qb) * ROWS + r * BLK
                qx[base : base + BLK, :] = jnp.concatenate([piece, marks], axis=1)
        scores(0)
        for i in range(2 * QBS):
            if i + 1 < 2 * QBS:
                scores(i + 1)
            weigh(b, i)
        for qb in range(QBS):
            c = comb[b, qb * BLK : (qb + 1) * BLK, :]
            c2 = c * c
            high = c2.astype(BF)
            low = (c2 - high.astype(F32)).astype(BF)
            e = jnp.ones((8, WIDTH), BF)
            total = dot(e, high, NT) + dot(e, low, NT)
            sq[b * QBS + qb] = total
        return carry

    lax.fori_loop(0, NSEQ, attend, 0)

    def sq_copy(d):
        return pltpu.make_async_remote_copy(
            src_ref=sq, dst_ref=sq_in.at[d - 1], send_sem=h_send.at[d - 1],
            recv_sem=h_recv.at[d - 1], device_id={"head": (hd + d) % NHEAD}, device_id_type=MESH,
        )

    for d in range(1, NHEAD):
        sq_copy(d).start()
    for d in range(1, NHEAD):
        sq_copy(d).wait_recv()

    eye = lax.broadcasted_iota(jnp.int32, (BLK, BLK), 0) == lax.broadcasted_iota(
        jnp.int32, (BLK, BLK), 1
    )
    scale_by = gain[...].astype(F32)

    def finish(n, carry):
        total = sq[n, 0:1, :]
        for d in range(1, NHEAD):
            total = total + sq_in[d - 1, n, 0:1, :]
        r = lax.rsqrt(total / (WIDTH * NHEAD) + epsilon)
        col = jnp.sum(jnp.where(eye, jnp.broadcast_to(r, (BLK, BLK)), 0.0), axis=1, keepdims=True)
        b, qb = n // QBS, n % QBS
        at = pl.ds(pl.multiple_of(qb * BLK, BLK), BLK)
        out_ref[b, at, :] = (comb[b, at, :] * col * scale_by).astype(BF)
        return carry

    lax.fori_loop(0, NSEQ * QBS, finish, 0)

    for d in range(1, NHEAD):
        sq_copy(d).wait_send()
    for o in range(2):
        for d in range(1, SIDE):
            pick_copy(o, d).wait_send()
            state_copy(o, d).wait_send()
    for b in range(NSEQ):
        for i in range(10):
            hop(b, i).wait_send()


def on_device(queries, keys_values, block_lists, starts, norm_gain):
    me = lax.axis_index("ctx")
    ctx = jnp.arange(NCTX, dtype=jnp.int32)
    owner = jnp.where(block_lists >= 0, block_lists // QBS, -1)
    hit = owner[..., None] == ctx
    picks = jnp.max(jnp.where(hit, (block_lists % QBS)[..., None], 0), axis=(1, 2))
    listed = jnp.any(hit, axis=2)
    own = jnp.any(
        block_lists[..., None] == me * QBS + jnp.arange(QBS, dtype=jnp.int32), axis=2
    )
    flags = jnp.concatenate([listed, own, jnp.zeros_like(own)], axis=2)
    flags = jnp.concatenate([flags, jnp.zeros_like(own)[..., :2]], axis=2)
    flags = jnp.where(flags, 0.0, NEG)
    bias = jnp.pad(
        jnp.transpose(flags, (0, 2, 1)), ((0, 0), (0, 0), (HD, LANES - HD - QBS))
    )
    pickrows = jnp.broadcast_to(
        picks.reshape(NSEQ * NCTX, 1).astype(F32), (NSEQ * NCTX, LANES)
    )
    smem = pl.BlockSpec(memory_space=pltpu.SMEM)
    vmem = pl.BlockSpec(memory_space=pltpu.VMEM)
    dma = pltpu.SemaphoreType.DMA
    return pl.pallas_call(
        kernel,
        in_specs=[smem, smem, pl.BlockSpec(memory_space=pl.ANY), vmem, vmem, vmem, vmem],
        out_specs=vmem,
        out_shape=jax.ShapeDtypeStruct((NSEQ, LEN, WIDTH), BF),
        scratch_shapes=[
            pltpu.VMEM((NSEQ, LEN, WIDTH), BF),
            pltpu.VMEM((NSEQ, 3, LEN, KVW), BF),
            pltpu.VMEM((NSEQ, 3, SIDE, BLK, KVW), BF),
            pltpu.VMEM((NSEQ, 3, SIDE, BLK, KVW), BF),
            pltpu.VMEM((NSEQ, 2, 2, BLK, KVW), BF),
            pltpu.VMEM((2, 3, NSEQ * NCTX, LANES), F32),
            pltpu.VMEM((NSEQ, 2, HD, LANES), BF),
            pltpu.VMEM((3, NSEQ, 2, HD, LANES), BF),
            pltpu.VMEM((NSEQ, 2, HD, LANES), BF),
            pltpu.VMEM((3, NSEQ, 2, HD, LANES), BF),
            pltpu.VMEM((NSEQ, 2, HD, LANES), F32),
            pltpu.VMEM((NSEQ, 2, LEN, LANES), BF),
            pltpu.VMEM((NSEQ, 2, LEN, LANES), BF),
            pltpu.VMEM((NSEQ, 2 * QBS, ROWS, LANES), F32),
            pltpu.VMEM((NSEQ, LEN, WIDTH), F32),
            pltpu.VMEM((2, SLOTS * BLK, LANES), BF),
            pltpu.VMEM((2, SLOTS * BLK, LANES), BF),
            pltpu.VMEM((2 * QBS * ROWS, LANES), BF),
            pltpu.VMEM((2, ROWS, LANES), BF),
            pltpu.VMEM((2, ROWS, SLOTS * BLK), F32),
            pltpu.VMEM((2, ROWS, SLOTS * BLK), BF),
            pltpu.VMEM((2, ROWS, LANES), F32),
            pltpu.VMEM((NSEQ * QBS, 8, LANES), F32),
            pltpu.VMEM((NHEAD - 1, NSEQ * QBS, 8, LANES), F32),
            dma,
            dma((NSEQ, 10)),
            dma((NSEQ, 10)),
            dma((6,)),
            dma((6,)),
            dma((6,)),
            dma((6,)),
            dma((NHEAD - 1,)),
            dma((NHEAD - 1,)),
        ],
        compiler_params=pltpu.CompilerParams(
            vmem_limit_bytes=60 << 20, collective_id=0, has_side_effects=True
        ),
    )(starts, picks, queries, keys_values, bias, pickrows, norm_gain.reshape(1, WIDTH))


def solution(mesh):
    return jax.shard_map(
        on_device,
        mesh=mesh,
        in_specs=(
            P(None, "ctx", "head"),
            P(None, "ctx", "head"),
            P(None, "ctx", None),
            P(),
            P("head"),
        ),
        out_specs=P(None, "ctx", "head"),
        check_vma=False,
    )
```

```python
import math

import jax
import jax.numpy as jnp
from jax import lax
from jax.experimental import pallas as pl
from jax.experimental.pallas import tpu as pltpu
from jax.sharding import PartitionSpec as P

HD = 96
BLK = 128
QBS = 3
TOPK = 16
NSEQ = 4
SIDE = 4
NCTX = 16
NHEAD = 8
GROUP = 4
LANES = 128
LEN = QBS * BLK
KVW = 4 * HD
WIDTH = 2 * GROUP * HD
ROWS = GROUP * BLK
HALF = BLK // 2
OWN0 = NCTX - 1
SLOTS = OWN0 + QBS
NCH = SLOTS // 2
TAIL = LANES - HD
epsilon = 1e-06
NEG = -1e30
SCALE = math.log2(math.e) / math.sqrt(HD)
NT = (((1,), (1,)), ((), ()))
TN = (((0,), (0,)), ((), ()))
NN = (((1,), (0,)), ((), ()))
BF = jnp.bfloat16
F32 = jnp.float32
MESH = pl.DeviceIdType.MESH


def dot(a, b, dims):
    return lax.dot_general(a, b, dims, preferred_element_type=F32)


def feature(x):
    x = x.astype(F32)
    return jnp.where(x > 0, x + 1.0, jnp.exp(jnp.minimum(x, 0.0)))


def kernel(
    starts, lists, q_hbm, kv, gain, out_ref,
    q_ref, near, packed, far, relay, bias_ref, pickrows, pk_in, st_own, st_y, st_row, st_x,
    prior, fk, vown, lin_ref, comb, kx, vx, qx, fq, sc, pw, mx, sq, sq_in,
    q_sem, s_send, s_recv, p_send, p_recv, t_send, t_recv, h_send, h_recv,
):
    me = lax.axis_index("ctx")
    hd = lax.axis_index("head")
    x, y = me // SIDE, me % SIDE

    def device(o, du, dv):
        dx, dy = (du, dv) if o == 0 else (dv, du)
        return ((x + dx + 2 * SIDE) % SIDE) * SIDE + (y + dy + 2 * SIDE) % SIDE

    def copy(src, dst, send, recv, target):
        return pltpu.make_async_remote_copy(
            src_ref=src, dst_ref=dst, send_sem=send, recv_sem=recv,
            device_id={"ctx": target}, device_id_type=MESH,
        )

    q_copy = pltpu.make_async_copy(q_hbm, q_ref, q_sem)
    q_copy.start()
    barrier = pltpu.get_barrier_semaphore()
    for o in range(2):
        for d in range(1, SIDE):
            pl.semaphore_signal(
                barrier, inc=1, device_id={"ctx": device(o, d, 0)}, device_id_type=MESH
            )
    for d in range(1, NHEAD):
        pl.semaphore_signal(
            barrier, inc=1, device_id={"head": (hd + d) % NHEAD}, device_id_type=MESH
        )
    pl.semaphore_wait(barrier, 2 * (SIDE - 1) + NHEAD - 1)

    def pick_copy(o, d):
        i = o * 3 + d - 1
        return copy(pickrows, pk_in.at[o, d - 1], p_send.at[i], p_recv.at[i], device(o, 0, -d))

    def hop(b, h, i):
        part = HALF // 2
        src, dst, du, dv = [
            (kv.at[b, :, h], near.at[b, h, 0], 1, 0),
            (kv.at[b, :, h], near.at[b, h, 2], -1, 0),
            (near.at[b, h, 0, :, 0:part], near.at[b, h, 1, :, 0:part], 1, 0),
            (near.at[b, h, 2, :, part:HALF], near.at[b, h, 1, :, part:HALF], -1, 0),
            (packed.at[b, h, 0], far.at[b, h, 0], 0, 1),
            (packed.at[b, h, 2], far.at[b, h, 2], 0, -1),
            (packed.at[b, h, 1, 0:2], relay.at[b, h, 0], 0, 1),
            (packed.at[b, h, 1, 2:4], relay.at[b, h, 1], 0, -1),
            (relay.at[b, h, 0], far.at[b, h, 1, 0:2], 0, 1),
            (relay.at[b, h, 1], far.at[b, h, 1, 2:4], 0, -1),
        ][i]
        return copy(src, dst, s_send.at[b, h, i], s_recv.at[b, h, i], device(h, du, dv))

    def start(b, *which):
        for i in which:
            for h in range(2):
                hop(b, h, i).start()

    def arrived(b, *which):
        for i in which:
            for h in range(2):
                hop(b, h, i).wait_recv()

    start(0, 0, 1)
    start(1, 0, 1)

    lane16 = lax.broadcasted_iota(jnp.int32, (NCTX, LANES), 1)
    lane8 = lax.broadcasted_iota(jnp.int32, (8, LANES), 1)
    of3 = lax.broadcasted_iota(jnp.int32, (NCTX, TOPK), 0) * QBS
    mine = lax.broadcasted_iota(jnp.int32, (8, TOPK), 0) + me * QBS
    for b in range(NSEQ):
        pick = jnp.zeros((NCTX, 1), F32)
        away = jnp.zeros((NCTX, LANES), F32)
        home = jnp.zeros((8, LANES), F32)
        for qb in range(QBS):
            entry = lists[b, qb : qb + 1, :]
            off = jnp.broadcast_to(entry, (NCTX, TOPK)) - of3
            hit = (off >= 0) & (off < QBS)
            named = jnp.max(jnp.where(hit, 1.0, 0.0), axis=1, keepdims=True)
            pick = jnp.maximum(
                pick, jnp.max(jnp.where(hit, off, 0).astype(F32), axis=1, keepdims=True)
            )
            away = jnp.where((lane16 == HD + qb) & (named < 0.5), NEG, away)
            held = jnp.broadcast_to(entry, (8, TOPK)) == mine
            named = jnp.max(jnp.where(held, 1.0, 0.0), axis=1, keepdims=True)
            home = jnp.where((lane8 == HD + qb) & (named < 0.5), NEG, home)
        bias_ref[b, 0:NCTX] = away
        bias_ref[b, NCTX : NCTX + 8] = home
        pickrows[b * NCTX : (b + 1) * NCTX] = jnp.broadcast_to(pick, (NCTX, LANES))
    for o in range(2):
        for d in range(1, SIDE):
            pick_copy(o, d).start()

    row96 = lax.broadcasted_iota(jnp.int32, (BLK, HD), 0)
    lane = lax.broadcasted_iota(jnp.int32, (BLK, TAIL), 1)
    row = lax.broadcasted_iota(jnp.int32, (BLK, TAIL), 0)
    zeros = jnp.zeros((BLK, TAIL), BF)
    ones = jnp.ones((BLK, TAIL), BF)

    def own_block(b, k, left, right):
        return jnp.concatenate([kv[b, k, 0, :, left:right], kv[b, k, 1, :, left:right]], axis=0)

    def summary(b, carry):
        first = starts[b]
        for k in range(QBS):
            at = slice(k * BLK, (k + 1) * BLK)
            live = row96 + (me * QBS + k) * BLK >= first
            for g in range(2):
                key = own_block(b, k, 2 * g * HD, (2 * g + 1) * HD)
                f = jnp.where(live, feature(key), 0.0).astype(BF)
                fk[b, g, at, :] = jnp.concatenate([f, zeros], axis=1)
                v = own_block(b, k, (2 * g + 1) * HD, (2 * g + 2) * HD)
                vown[b, g, at, :] = jnp.concatenate([v, ones], axis=1)
        for g in range(2):
            t = dot(fk[b, g], vown[b, g], TN)
            st_own[b, g] = t[:HD].astype(BF)
        return carry

    lax.fori_loop(0, NSEQ, summary, 0)

    def state_copy(o, i):
        own, got = (st_row, st_x) if o == 0 else (st_own, st_y)
        part = NSEQ // 2
        src, dst, du = [
            (own, got.at[0], 1),
            (own, got.at[2], -1),
            (got.at[0, 0:part], got.at[1, 0:part], 1),
            (got.at[2, part:NSEQ], got.at[1, part:NSEQ], -1),
        ][i]
        return copy(src, dst, t_send.at[o, i], t_recv.at[o, i], device(o, du, 0))

    def pass_on(b):
        arrived(b, 0, 1)
        start(b, 2, 3)

    def relay_on(b):
        arrived(b, 6, 7)
        start(b, 8, 9)

    def source(o, du, dv):
        return device(o, -du, -dv)

    def choose(table, at, blocks):
        w = jnp.broadcast_to(table[pl.ds(at, 1), :], (HALF, LANES)).astype(BF)
        m0, m1 = w == 0.0, w == 1.0
        out = []
        for c in range(KVW // LANES):
            b0, b1, b2 = [blocks[k, :, c * LANES : (c + 1) * LANES] for k in range(QBS)]
            out.append(jnp.where(m0, b0, jnp.where(m1, b1, b2)))
        return jnp.concatenate(out, axis=1)

    def pack(b):
        arrived(b, 2, 3)
        for h in range(2):
            for dv in range(1, SIDE):
                for du in range(SIDE):
                    blocks = kv.at[b, :, h] if du == 0 else near.at[b, h, du - 1]
                    packed[b, h, dv - 1, du] = choose(
                        pk_in.at[h, dv - 1], b * NCTX + source(h, du, 0), blocks
                    )
        start(b, 6, 7, 4, 5)

    for i in (0, 1):
        state_copy(1, i).start()
    pass_on(0)
    pass_on(1)
    for i in (0, 1):
        state_copy(1, i).wait_recv()
    for i in (2, 3):
        state_copy(1, i).start()
    for o in range(2):
        for d in range(1, SIDE):
            pick_copy(o, d).wait_recv()
    pack(0)
    for i in (2, 3):
        state_copy(1, i).wait_recv()

    def rows_sum(b, carry):
        for g in range(2):
            total = st_own[b, g].astype(F32)
            before = jnp.zeros((HD, LANES), F32)
            for d in range(1, SIDE):
                part = st_y[d - 1, b, g].astype(F32)
                total = total + part
                before = before + jnp.where(y >= d, part, 0.0)
            st_row[b, g] = total.astype(BF)
            prior[b, g] = before
        return carry

    lax.fori_loop(0, NSEQ, rows_sum, 0)
    for i in (0, 1):
        state_copy(0, i).start()
    start(2, 0, 1)
    pack(1)
    start(3, 0, 1)
    relay_on(0)
    for i in (0, 1):
        state_copy(0, i).wait_recv()
    for i in (2, 3):
        state_copy(0, i).start()
    pass_on(2)
    q_copy.wait()
    for i in (2, 3):
        state_copy(0, i).wait_recv()

    def add_x(b, carry):
        for g in range(2):
            before = prior[b, g]
            for d in range(1, SIDE):
                before = before + jnp.where(x >= d, st_x[d - 1, b, g].astype(F32), 0.0)
            prior[b, g] = before
        return carry

    lax.fori_loop(0, NSEQ, add_x, 0)

    trow = lax.broadcasted_iota(jnp.int32, (ROWS, BLK), 0) % BLK
    tlane = lax.broadcasted_iota(jnp.int32, (ROWS, BLK), 1)
    causal = trow >= tlane

    def live_rows(b, qb):
        r = lax.broadcasted_iota(jnp.int32, (ROWS, 1), 0) % BLK
        return r + (me * QBS + qb) * BLK >= starts[b]

    def linear(b):
        for g in range(2):
            state = jnp.concatenate([prior[b, g], jnp.zeros((TAIL, LANES), F32)], axis=0)
            for qb in range(QBS):
                marks = jnp.where((lane == qb) | (lane == QBS), 1.0, 0.0).astype(BF)
                base = (g * QBS + qb) * ROWS
                for h in range(GROUP):
                    c = (g * GROUP + h) * HD
                    piece = q_ref[b, qb * BLK : (qb + 1) * BLK, c : c + HD]
                    fq[qb % 2, h * BLK : (h + 1) * BLK, :] = jnp.concatenate(
                        [feature(piece).astype(BF), zeros], axis=1
                    )
                    qx[base + h * BLK : base + (h + 1) * BLK, :] = jnp.concatenate(
                        [piece, marks], axis=1
                    )
                fqv = fq[qb % 2]
                fkv = fk[b, g, qb * BLK : (qb + 1) * BLK, :]
                vo = vown[b, g, qb * BLK : (qb + 1) * BLK, :]
                inner = jnp.where(causal, dot(fqv, fkv, NT), 0.0).astype(BF)
                high = state.astype(BF)
                low = (state - high.astype(F32)).astype(BF)
                lin = dot(inner, vo, NN) + dot(fqv, high, NN) + dot(fqv, low, NN)
                if qb < QBS - 1:
                    state = state + dot(fkv, vo, TN)
                den = jnp.where(live_rows(b, qb), lin[:, HD : HD + 1], 1.0)
                lin_ref[g * QBS + qb] = lin * (1.0 / den)

    def place(first, count, load, bias):
        at = slice(first, first + count)
        for g in range(2):
            k = load(2 * g * HD, (2 * g + 1) * HD)
            v = load((2 * g + 1) * HD, (2 * g + 2) * HD)
            kx[g, at, :] = jnp.concatenate([k, bias], axis=1)
            vx[g, at, :] = jnp.concatenate([v, ones[:count]], axis=1)

    def tail_bias(b, slot_row, pos):
        listed = bias_ref[b, pl.ds(slot_row, 1), HD:LANES]
        late = jnp.where((lane == QBS) & (row.astype(F32) + pos < starts[b].astype(F32)), NEG, 0.0)
        return (listed + late).astype(BF)

    def scores(i):
        g, qb = i // QBS, i % QBS
        q = qx[i * ROWS : (i + 1) * ROWS, :]
        top = None
        for c in range(NCH):
            at = slice(c * 2 * BLK, (c + 1) * 2 * BLK)
            s = dot(q, kx[g, at, :], NT)
            parts = []
            for n in range(2):
                k = 2 * c + n - OWN0
                part = s[:, n * BLK : (n + 1) * BLK]
                if k == qb:
                    part = jnp.where(causal, part, NEG)
                parts.append(part)
                sc[i % 2, :, (2 * c + n) * BLK : (2 * c + n + 1) * BLK] = part
            t = jnp.maximum(parts[0], parts[1])
            top = t if top is None else jnp.maximum(top, t)
        mx[i % 2] = top

    def weigh(b, i):
        g, qb = i // QBS, i % QBS
        peak = jnp.max(mx[i % 2], axis=1, keepdims=True)
        for c in range(NCH):
            at = slice(c * 2 * BLK, (c + 1) * 2 * BLK)
            pw[i % 2, :, at] = jnp.exp2((sc[i % 2, :, at] - peak) * SCALE).astype(BF)
        acc = dot(pw[i % 2], vx[g], NN)
        both = lin_ref[i] + acc * (1.0 / acc[:, HD : HD + 1])
        both = jnp.where(live_rows(b, qb), both, 0.0)
        comb[b, qb * BLK : (qb + 1) * BLK, g * GROUP * HD : (g + 1) * GROUP * HD] = (
            jnp.concatenate([both[h * BLK : (h + 1) * BLK, :HD] for h in range(GROUP)], axis=1)
        )

    def attend(b, carry):
        linear(b)
        arrived(b, 4, 5, 8, 9)
        slot = 0
        for dx in range(SIDE):
            for dy in range(SIDE):
                if dx == 0 and dy == 0:
                    continue
                s = source(0, dx, dy)
                at = b * NCTX + s
                pos = (pickrows[pl.ds(at, 1), HD:LANES] + (s * QBS).astype(F32)) * BLK
                tb = tail_bias(b, s, pos)
                for h in range(2):
                    du, dv = (dx, dy) if h == 0 else (dy, dx)
                    if dv == 0:
                        whole = choose(pickrows, at, near.at[b, h, du - 1])
                    else:
                        whole = far[b, h, dv - 1, du]
                    place(
                        slot * BLK + h * HALF, HALF, lambda l, r, w=whole: w[:, l:r],
                        tb[h * HALF : (h + 1) * HALF],
                    )
                slot += 1
        for k in range(QBS):
            pos = ((me * QBS + k) * BLK).astype(F32)
            tb = tail_bias(b, NCTX + k, pos)
            place(slot * BLK, BLK, lambda l, r, k=k: own_block(b, k, l, r), tb)
            slot += 1
        scores(0)
        for i in range(QBS):
            if i + 1 < QBS:
                scores(i + 1)
            weigh(b, i)

        for c in range(NSEQ - 1):

            @pl.when(b == c)
            def _(c=c):
                relay_on(c + 1)
                if c + 2 < NSEQ:
                    pack(c + 2)
                if c == 0:
                    pass_on(3)

        scores(QBS)
        for i in range(QBS, 2 * QBS):
            if i + 1 < 2 * QBS:
                scores(i + 1)
            weigh(b, i)
        for qb in range(QBS):
            c = comb[b, qb * BLK : (qb + 1) * BLK, :]
            c2 = c * c
            high = c2.astype(BF)
            low = (c2 - high.astype(F32)).astype(BF)
            e = jnp.ones((8, WIDTH), BF)
            sq[b * QBS + qb] = dot(e, high, NT) + dot(e, low, NT)
        return carry

    lax.fori_loop(0, NSEQ, attend, 0)

    def sq_copy(d):
        return pltpu.make_async_remote_copy(
            src_ref=sq, dst_ref=sq_in.at[d - 1], send_sem=h_send.at[d - 1],
            recv_sem=h_recv.at[d - 1], device_id={"head": (hd + d) % NHEAD}, device_id_type=MESH,
        )

    for d in range(1, NHEAD):
        sq_copy(d).start()
    for d in range(1, NHEAD):
        sq_copy(d).wait_recv()

    eye = lax.broadcasted_iota(jnp.int32, (BLK, BLK), 0) == lax.broadcasted_iota(
        jnp.int32, (BLK, BLK), 1
    )
    scale_by = gain[...].astype(F32).reshape(1, WIDTH)

    def finish(n, carry):
        total = sq[n, 0:1, :]
        for d in range(1, NHEAD):
            total = total + sq_in[d - 1, n, 0:1, :]
        r = lax.rsqrt(total / (WIDTH * NHEAD) + epsilon)
        col = jnp.sum(jnp.where(eye, jnp.broadcast_to(r, (BLK, BLK)), 0.0), axis=1, keepdims=True)
        b, qb = n // QBS, n % QBS
        at = pl.ds(pl.multiple_of(qb * BLK, BLK), BLK)
        out_ref[b, at, :] = (comb[b, at, :] * col * scale_by).astype(BF)
        return carry

    lax.fori_loop(0, NSEQ * QBS, finish, 0)

    for d in range(1, NHEAD):
        sq_copy(d).wait_send()
    for o in range(2):
        for d in range(1, SIDE):
            pick_copy(o, d).wait_send()
        for i in range(4):
            state_copy(o, i).wait_send()
    for b in range(NSEQ):
        for h in range(2):
            for i in range(10):
                hop(b, h, i).wait_send()


def on_device(queries, keys_values, block_lists, starts, norm_gain):
    smem = pl.BlockSpec(memory_space=pltpu.SMEM)
    vmem = pl.BlockSpec(memory_space=pltpu.VMEM)
    dma = pltpu.SemaphoreType.DMA
    return pl.pallas_call(
        kernel,
        in_specs=[smem, vmem, pl.BlockSpec(memory_space=pl.ANY), vmem, vmem],
        out_specs=vmem,
        out_shape=jax.ShapeDtypeStruct((NSEQ, LEN, WIDTH), BF),
        scratch_shapes=[
            pltpu.VMEM((NSEQ, LEN, WIDTH), BF),
            pltpu.VMEM((NSEQ, 2, 3, QBS, HALF, KVW), BF),
            pltpu.VMEM((NSEQ, 2, 3, SIDE, HALF, KVW), BF),
            pltpu.VMEM((NSEQ, 2, 3, SIDE, HALF, KVW), BF),
            pltpu.VMEM((NSEQ, 2, 2, 2, HALF, KVW), BF),
            pltpu.VMEM((NSEQ, NCTX + 8, LANES), F32),
            pltpu.VMEM((NSEQ * NCTX, LANES), F32),
            pltpu.VMEM((2, 3, NSEQ * NCTX, LANES), F32),
            pltpu.VMEM((NSEQ, 2, HD, LANES), BF),
            pltpu.VMEM((3, NSEQ, 2, HD, LANES), BF),
            pltpu.VMEM((NSEQ, 2, HD, LANES), BF),
            pltpu.VMEM((3, NSEQ, 2, HD, LANES), BF),
            pltpu.VMEM((NSEQ, 2, HD, LANES), F32),
            pltpu.VMEM((NSEQ, 2, LEN, LANES), BF),
            pltpu.VMEM((NSEQ, 2, LEN, LANES), BF),
            pltpu.VMEM((2 * QBS, ROWS, LANES), F32),
            pltpu.VMEM((NSEQ, LEN, WIDTH), F32),
            pltpu.VMEM((2, SLOTS * BLK, LANES), BF),
            pltpu.VMEM((2, SLOTS * BLK, LANES), BF),
            pltpu.VMEM((2 * QBS * ROWS, LANES), BF),
            pltpu.VMEM((2, ROWS, LANES), BF),
            pltpu.VMEM((2, ROWS, SLOTS * BLK), F32),
            pltpu.VMEM((2, ROWS, SLOTS * BLK), BF),
            pltpu.VMEM((2, ROWS, LANES), F32),
            pltpu.VMEM((NSEQ * QBS, 8, LANES), F32),
            pltpu.VMEM((NHEAD - 1, NSEQ * QBS, 8, LANES), F32),
            dma,
            dma((NSEQ, 2, 10)),
            dma((NSEQ, 2, 10)),
            dma((6,)),
            dma((6,)),
            dma((2, 4)),
            dma((2, 4)),
            dma((NHEAD - 1,)),
            dma((NHEAD - 1,)),
        ],
        compiler_params=pltpu.CompilerParams(
            vmem_limit_bytes=60 << 20, collective_id=0, has_side_effects=True
        ),
    )(
        starts,
        block_lists,
        queries,
        keys_values.reshape(NSEQ, QBS, 2, HALF, KVW),
        norm_gain,
    )


def solution(mesh):
    return jax.shard_map(
        on_device,
        mesh=mesh,
        in_specs=(
            P(None, "ctx", "head"),
            P(None, "ctx", "head"),
            P(None, "ctx", None),
            P(),
            P("head"),
        ),
        out_specs=P(None, "ctx", "head"),
        check_vma=False,
    )
```

```python
import math

import jax
import jax.numpy as jnp
from jax import lax
from jax.experimental import pallas as pl
from jax.experimental.pallas import tpu as pltpu
from jax.sharding import PartitionSpec as P

HD = 96
BLK = 128
QBS = 3
TOPK = 16
NSEQ = 4
SIDE = 4
NCTX = 16
NHEAD = 8
GROUP = 4
LANES = 128
LEN = QBS * BLK
KVW = 4 * HD
WIDTH = 2 * GROUP * HD
ROWS = GROUP * BLK
HALF = BLK // 2
OWN0 = NCTX - 1
SLOTS = OWN0 + QBS
NCH = SLOTS // 2
TAIL = LANES - HD
epsilon = 1e-06
NEG = -1e30
SCALE = math.log2(math.e) / math.sqrt(HD)
NT = (((1,), (1,)), ((), ()))
TN = (((0,), (0,)), ((), ()))
NN = (((1,), (0,)), ((), ()))
BF = jnp.bfloat16
F32 = jnp.float32
MESH = pl.DeviceIdType.MESH


def dot(a, b, dims):
    return lax.dot_general(a, b, dims, preferred_element_type=F32)


def feature(x):
    x = x.astype(F32)
    return jnp.where(x > 0, x + 1.0, jnp.exp(jnp.minimum(x, 0.0)))


def kernel(
    starts, lists, q_hbm, kv, gain, out_hbm,
    q_ref, near, packed, far, relay, bias_ref, pickrows, pickpack, pk_raw, pk_in, st_own, st_y, st_row, st_x,
    prior, fk, vown, lin_ref, comb, kx, vx, qx, fq, sc, pw, mx, sq, sq_in,
    out_ref, out_sem, q_sem, s_send, s_recv, p_send, p_recv, t_send, t_recv, h_send, h_recv,
):
    me = lax.axis_index("ctx")
    hd = lax.axis_index("head")
    x, y = me // SIDE, me % SIDE

    def device(o, du, dv):
        dx, dy = (du, dv) if o == 0 else (dv, du)
        return ((x + dx + 2 * SIDE) % SIDE) * SIDE + (y + dy + 2 * SIDE) % SIDE

    def copy(src, dst, send, recv, target):
        return pltpu.make_async_remote_copy(
            src_ref=src, dst_ref=dst, send_sem=send, recv_sem=recv,
            device_id={"ctx": target}, device_id_type=MESH,
        )

    q_copy = pltpu.make_async_copy(q_hbm, q_ref, q_sem)
    q_copy.start()
    barrier = pltpu.get_barrier_semaphore()
    for o in range(2):
        for d in range(1, SIDE):
            pl.semaphore_signal(
                barrier, inc=1, device_id={"ctx": device(o, d, 0)}, device_id_type=MESH
            )
    for d in range(1, NHEAD):
        pl.semaphore_signal(
            barrier, inc=1, device_id={"head": (hd + d) % NHEAD}, device_id_type=MESH
        )
    pl.semaphore_wait(barrier, 2 * (SIDE - 1) + NHEAD - 1)

    def pick_copy(o, d):
        i = o * 3 + d - 1
        return copy(pickpack, pk_raw.at[o, d - 1], p_send.at[i], p_recv.at[i], device(o, 0, -d))

    def hop(b, h, i):
        part = HALF // 2
        src, dst, du, dv = [
            (kv.at[b, :, h], near.at[b, h, 0], 1, 0),
            (kv.at[b, :, h], near.at[b, h, 2], -1, 0),
            (near.at[b, h, 0, :, 0:part], near.at[b, h, 1, :, 0:part], 1, 0),
            (near.at[b, h, 2, :, part:HALF], near.at[b, h, 1, :, part:HALF], -1, 0),
            (packed.at[b, h, 0], far.at[b, h, 0], 0, 1),
            (packed.at[b, h, 2], far.at[b, h, 2], 0, -1),
            (packed.at[b, h, 1, 0:2], relay.at[b, h, 0], 0, 1),
            (packed.at[b, h, 1, 2:4], relay.at[b, h, 1], 0, -1),
            (relay.at[b, h, 0], far.at[b, h, 1, 0:2], 0, 1),
            (relay.at[b, h, 1], far.at[b, h, 1, 2:4], 0, -1),
        ][i]
        return copy(src, dst, s_send.at[b, h, i], s_recv.at[b, h, i], device(h, du, dv))

    def start(b, *which):
        for i in which:
            for h in range(2):
                hop(b, h, i).start()

    def arrived(b, *which):
        for i in which:
            for h in range(2):
                hop(b, h, i).wait_recv()

    start(0, 0, 1)
    start(1, 0, 1)

    lane16 = lax.broadcasted_iota(jnp.int32, (NCTX, LANES), 1)
    lane8 = lax.broadcasted_iota(jnp.int32, (8, LANES), 1)
    match = lane16 == lax.broadcasted_iota(jnp.int32, (NCTX, LANES), 0)
    pickpack[...] = jnp.zeros((8, LANES), F32)
    sq[...] = jnp.zeros((16, LANES), F32)
    of3 = lax.broadcasted_iota(jnp.int32, (NCTX, TOPK), 0) * QBS
    mine = lax.broadcasted_iota(jnp.int32, (8, TOPK), 0) + me * QBS
    for b in range(NSEQ):
        pick = jnp.zeros((NCTX, 1), F32)
        away = jnp.zeros((NCTX, LANES), F32)
        home = jnp.zeros((8, LANES), F32)
        for qb in range(QBS):
            entry = lists[b, qb : qb + 1, :]
            off = jnp.broadcast_to(entry, (NCTX, TOPK)) - of3
            hit = (off >= 0) & (off < QBS)
            named = jnp.max(jnp.where(hit, 1.0, 0.0), axis=1, keepdims=True)
            pick = jnp.maximum(
                pick, jnp.max(jnp.where(hit, off, 0).astype(F32), axis=1, keepdims=True)
            )
            away = jnp.where((lane16 == HD + qb) & (named < 0.5), NEG, away)
            held = jnp.broadcast_to(entry, (8, TOPK)) == mine
            named = jnp.max(jnp.where(held, 1.0, 0.0), axis=1, keepdims=True)
            home = jnp.where((lane8 == HD + qb) & (named < 0.5), NEG, home)
        bias_ref[b, 0:NCTX] = away
        bias_ref[b, NCTX : NCTX + 8] = home
        spread = jnp.broadcast_to(pick, (NCTX, LANES))
        pickrows[b * NCTX : (b + 1) * NCTX] = spread
        pickpack[b : b + 1, :] = jnp.sum(jnp.where(match, spread, 0.0), axis=0, keepdims=True)
    for o in range(2):
        for d in range(1, SIDE):
            pick_copy(o, d).start()

    row96 = lax.broadcasted_iota(jnp.int32, (BLK, HD), 0)
    lane = lax.broadcasted_iota(jnp.int32, (BLK, TAIL), 1)
    row = lax.broadcasted_iota(jnp.int32, (BLK, TAIL), 0)
    zeros = jnp.zeros((BLK, TAIL), BF)
    ones = jnp.ones((BLK, TAIL), BF)

    def own_block(b, k, left, right):
        return jnp.concatenate([kv[b, k, 0, :, left:right], kv[b, k, 1, :, left:right]], axis=0)

    def summary(b, carry):
        first = starts[b]
        for k in range(QBS):
            at = slice(k * BLK, (k + 1) * BLK)
            live = row96 + (me * QBS + k) * BLK >= first
            for g in range(2):
                key = own_block(b, k, 2 * g * HD, (2 * g + 1) * HD)
                f = jnp.where(live, feature(key), 0.0).astype(BF)
                fk[b, g, at, :] = jnp.concatenate([f, zeros], axis=1)
                v = own_block(b, k, (2 * g + 1) * HD, (2 * g + 2) * HD)
                vown[b, g, at, :] = jnp.concatenate([v, ones], axis=1)
        for g in range(2):
            t = dot(fk[b, g], vown[b, g], TN)
            st_own[b, g] = t[:HD].astype(BF)
        return carry

    lax.fori_loop(0, NSEQ, summary, 0)

    def state_copy(o, i):
        own, got = (st_row, st_x) if o == 0 else (st_own, st_y)
        part = NSEQ // 2
        src, dst, du = [
            (own, got.at[0], 1),
            (own, got.at[2], -1),
            (got.at[0, 0:part], got.at[1, 0:part], 1),
            (got.at[2, part:NSEQ], got.at[1, part:NSEQ], -1),
        ][i]
        return copy(src, dst, t_send.at[o, i], t_recv.at[o, i], device(o, du, 0))

    def pass_on(b):
        arrived(b, 0, 1)
        start(b, 2, 3)

    def relay_on(b):
        arrived(b, 6, 7)
        start(b, 8, 9)

    def source(o, du, dv):
        return device(o, -du, -dv)

    def choose(table, at, blocks):
        w = jnp.broadcast_to(table[pl.ds(at, 1), :], (HALF, LANES)).astype(BF)
        m0, m1 = w == 0.0, w == 1.0
        out = []
        for c in range(KVW // LANES):
            b0, b1, b2 = [blocks[k, :, c * LANES : (c + 1) * LANES] for k in range(QBS)]
            out.append(jnp.where(m0, b0, jnp.where(m1, b1, b2)))
        return jnp.concatenate(out, axis=1)

    def pack(b):
        arrived(b, 2, 3)
        for h in range(2):
            for dv in range(1, SIDE):
                for du in range(SIDE):
                    blocks = kv.at[b, :, h] if du == 0 else near.at[b, h, du - 1]
                    packed[b, h, dv - 1, du] = choose(
                        pk_in.at[h, dv - 1], b * NCTX + source(h, du, 0), blocks
                    )
        start(b, 6, 7, 4, 5)

    for i in (0, 1):
        state_copy(1, i).start()
    pass_on(0)
    pass_on(1)
    for i in (0, 1):
        state_copy(1, i).wait_recv()
    for i in (2, 3):
        state_copy(1, i).start()
    for o in range(2):
        for d in range(1, SIDE):
            pick_copy(o, d).wait_recv()
            for b in range(NSEQ):
                line = jnp.broadcast_to(pk_raw[o, d - 1, b : b + 1, :], (NCTX, LANES))
                col = jnp.sum(jnp.where(match, line, 0.0), axis=1, keepdims=True)
                pk_in[o, d - 1, b * NCTX : (b + 1) * NCTX] = jnp.broadcast_to(col, (NCTX, LANES))
    pack(0)
    for i in (2, 3):
        state_copy(1, i).wait_recv()

    def rows_sum(b, carry):
        for g in range(2):
            total = st_own[b, g].astype(F32)
            before = jnp.zeros((HD, LANES), F32)
            for d in range(1, SIDE):
                part = st_y[d - 1, b, g].astype(F32)
                total = total + part
                before = before + jnp.where(y >= d, part, 0.0)
            st_row[b, g] = total.astype(BF)
            prior[b, g] = before
        return carry

    lax.fori_loop(0, NSEQ, rows_sum, 0)
    for i in (0, 1):
        state_copy(0, i).start()
    start(2, 0, 1)
    pack(1)
    start(3, 0, 1)
    relay_on(0)
    for i in (0, 1):
        state_copy(0, i).wait_recv()
    for i in (2, 3):
        state_copy(0, i).start()
    pass_on(2)
    q_copy.wait()
    for i in (2, 3):
        state_copy(0, i).wait_recv()

    def add_x(b, carry):
        for g in range(2):
            before = prior[b, g]
            for d in range(1, SIDE):
                before = before + jnp.where(x >= d, st_x[d - 1, b, g].astype(F32), 0.0)
            prior[b, g] = before
        return carry

    lax.fori_loop(0, NSEQ, add_x, 0)

    trow = lax.broadcasted_iota(jnp.int32, (ROWS, BLK), 0) % BLK
    tlane = lax.broadcasted_iota(jnp.int32, (ROWS, BLK), 1)
    causal = trow >= tlane

    def live_rows(b, qb):
        r = lax.broadcasted_iota(jnp.int32, (ROWS, 1), 0) % BLK
        return r + (me * QBS + qb) * BLK >= starts[b]

    def linear(b):
        for g in range(2):
            state = jnp.concatenate([prior[b, g], jnp.zeros((TAIL, LANES), F32)], axis=0)
            for qb in range(QBS):
                marks = jnp.where((lane == qb) | (lane == QBS), 1.0, 0.0).astype(BF)
                base = (g * QBS + qb) * ROWS
                for h in range(GROUP):
                    c = (g * GROUP + h) * HD
                    piece = q_ref[b, qb * BLK : (qb + 1) * BLK, c : c + HD]
                    fq[qb % 2, h * BLK : (h + 1) * BLK, :] = jnp.concatenate(
                        [feature(piece).astype(BF), zeros], axis=1
                    )
                    qx[base + h * BLK : base + (h + 1) * BLK, :] = jnp.concatenate(
                        [piece, marks], axis=1
                    )
                fqv = fq[qb % 2]
                fkv = fk[b, g, qb * BLK : (qb + 1) * BLK, :]
                vo = vown[b, g, qb * BLK : (qb + 1) * BLK, :]
                inner = jnp.where(causal, dot(fqv, fkv, NT), 0.0).astype(BF)
                high = state.astype(BF)
                low = (state - high.astype(F32)).astype(BF)
                lin = dot(inner, vo, NN) + dot(fqv, high, NN) + dot(fqv, low, NN)
                if qb < QBS - 1:
                    state = state + dot(fkv, vo, TN)
                den = jnp.where(live_rows(b, qb), lin[:, HD : HD + 1], 1.0)
                lin_ref[g * QBS + qb] = lin * (1.0 / den)

    def place(first, count, load, bias):
        at = slice(first, first + count)
        for g in range(2):
            k = load(2 * g * HD, (2 * g + 1) * HD)
            v = load((2 * g + 1) * HD, (2 * g + 2) * HD)
            kx[g, at, :] = jnp.concatenate([k, bias], axis=1)
            vx[g, at, :] = jnp.concatenate([v, ones[:count]], axis=1)

    def tail_bias(b, slot_row, pos):
        listed = bias_ref[b, pl.ds(slot_row, 1), HD:LANES]
        late = jnp.where((lane == QBS) & (row.astype(F32) + pos < starts[b].astype(F32)), NEG, 0.0)
        return (listed + late).astype(BF)

    def scores(i):
        g, qb = i // QBS, i % QBS
        q = qx[i * ROWS : (i + 1) * ROWS, :]
        top = None
        for c in range(NCH):
            at = slice(c * 2 * BLK, (c + 1) * 2 * BLK)
            s = dot(q, kx[g, at, :], NT)
            parts = []
            for n in range(2):
                k = 2 * c + n - OWN0
                part = s[:, n * BLK : (n + 1) * BLK]
                if k == qb:
                    part = jnp.where(causal, part, NEG)
                parts.append(part)
                sc[i % 2, :, (2 * c + n) * BLK : (2 * c + n + 1) * BLK] = part
            t = jnp.maximum(parts[0], parts[1])
            top = t if top is None else jnp.maximum(top, t)
        mx[i % 2] = top

    def weigh(b, i):
        g, qb = i // QBS, i % QBS
        peak = jnp.max(mx[i % 2], axis=1, keepdims=True)
        for c in range(NCH):
            at = slice(c * 2 * BLK, (c + 1) * 2 * BLK)
            pw[i % 2, :, at] = jnp.exp2((sc[i % 2, :, at] - peak) * SCALE).astype(BF)
        acc = dot(pw[i % 2], vx[g], NN)
        both = lin_ref[i] + acc * (1.0 / acc[:, HD : HD + 1])
        both = jnp.where(live_rows(b, qb), both, 0.0)
        comb[b, qb * BLK : (qb + 1) * BLK, g * GROUP * HD : (g + 1) * GROUP * HD] = (
            jnp.concatenate([both[h * BLK : (h + 1) * BLK, :HD] for h in range(GROUP)], axis=1)
        )

    def attend(b, carry):
        linear(b)
        arrived(b, 4, 5, 8, 9)
        slot = 0
        for dx in range(SIDE):
            for dy in range(SIDE):
                if dx == 0 and dy == 0:
                    continue
                s = source(0, dx, dy)
                at = b * NCTX + s
                pos = (pickrows[pl.ds(at, 1), HD:LANES] + (s * QBS).astype(F32)) * BLK
                tb = tail_bias(b, s, pos)
                for h in range(2):
                    du, dv = (dx, dy) if h == 0 else (dy, dx)
                    if dv == 0:
                        whole = choose(pickrows, at, near.at[b, h, du - 1])
                    else:
                        whole = far[b, h, dv - 1, du]
                    place(
                        slot * BLK + h * HALF, HALF, lambda l, r, w=whole: w[:, l:r],
                        tb[h * HALF : (h + 1) * HALF],
                    )
                slot += 1
        for k in range(QBS):
            pos = ((me * QBS + k) * BLK).astype(F32)
            tb = tail_bias(b, NCTX + k, pos)
            place(slot * BLK, BLK, lambda l, r, k=k: own_block(b, k, l, r), tb)
            slot += 1
        scores(0)
        for i in range(QBS):
            if i + 1 < QBS:
                scores(i + 1)
            weigh(b, i)

        for c in range(NSEQ - 1):

            @pl.when(b == c)
            def _(c=c):
                relay_on(c + 1)
                if c + 2 < NSEQ:
                    pack(c + 2)
                if c == 0:
                    pass_on(3)

        scores(QBS)
        for i in range(QBS, 2 * QBS):
            if i + 1 < 2 * QBS:
                scores(i + 1)
            weigh(b, i)
        for qb in range(QBS):
            c = comb[b, qb * BLK : (qb + 1) * BLK, :]
            c2 = c * c
            high = c2.astype(BF)
            low = (c2 - high.astype(F32)).astype(BF)
            e = jnp.ones((8, WIDTH), BF)
            sq[pl.ds(b * QBS + qb, 1), :] = (dot(e, high, NT) + dot(e, low, NT))[0:1]
        return carry

    lax.fori_loop(0, NSEQ, attend, 0)

    def sq_copy(d):
        return pltpu.make_async_remote_copy(
            src_ref=sq, dst_ref=sq_in.at[d - 1], send_sem=h_send.at[d - 1],
            recv_sem=h_recv.at[d - 1], device_id={"head": (hd + d) % NHEAD}, device_id_type=MESH,
        )

    for d in range(1, NHEAD):
        sq_copy(d).start()
    for d in range(1, NHEAD):
        sq_copy(d).wait_recv()

    eye = lax.broadcasted_iota(jnp.int32, (BLK, BLK), 0) == lax.broadcasted_iota(
        jnp.int32, (BLK, BLK), 1
    )
    scale_by = gain[...].astype(F32).reshape(1, WIDTH)

    def out_copy(n):
        rows = pl.ds(pl.multiple_of(n % QBS * BLK, BLK), BLK) if not isinstance(n, int) else pl.ds(n % QBS * BLK, BLK)
        return pltpu.make_async_copy(out_ref.at[n], out_hbm.at[n // QBS, rows], out_sem.at[n])

    def finish(n, carry):
        total = sq[pl.ds(n, 1), :]
        for d in range(1, NHEAD):
            total = total + sq_in[d - 1, pl.ds(n, 1), :]
        r = lax.rsqrt(total / (WIDTH * NHEAD) + epsilon)
        col = jnp.sum(jnp.where(eye, jnp.broadcast_to(r, (BLK, BLK)), 0.0), axis=1, keepdims=True)
        b, qb = n // QBS, n % QBS
        at = pl.ds(pl.multiple_of(qb * BLK, BLK), BLK)
        out_ref[n] = (comb[b, at, :] * col * scale_by).astype(BF)
        out_copy(n).start()
        return carry

    lax.fori_loop(0, NSEQ * QBS, finish, 0)
    for n in range(NSEQ * QBS):
        out_copy(n).wait()

    for d in range(1, NHEAD):
        sq_copy(d).wait_send()
    for o in range(2):
        for d in range(1, SIDE):
            pick_copy(o, d).wait_send()
        for i in range(4):
            state_copy(o, i).wait_send()
    for b in range(NSEQ):
        for h in range(2):
            for i in range(10):
                hop(b, h, i).wait_send()


def on_device(queries, keys_values, block_lists, starts, norm_gain):
    smem = pl.BlockSpec(memory_space=pltpu.SMEM)
    vmem = pl.BlockSpec(memory_space=pltpu.VMEM)
    dma = pltpu.SemaphoreType.DMA
    return pl.pallas_call(
        kernel,
        in_specs=[smem, vmem, pl.BlockSpec(memory_space=pl.ANY), vmem, vmem],
        out_specs=pl.BlockSpec(memory_space=pl.ANY),
        out_shape=jax.ShapeDtypeStruct((NSEQ, LEN, WIDTH), BF),
        scratch_shapes=[
            pltpu.VMEM((NSEQ, LEN, WIDTH), BF),
            pltpu.VMEM((NSEQ, 2, 3, QBS, HALF, KVW), BF),
            pltpu.VMEM((NSEQ, 2, 3, SIDE, HALF, KVW), BF),
            pltpu.VMEM((NSEQ, 2, 3, SIDE, HALF, KVW), BF),
            pltpu.VMEM((NSEQ, 2, 2, 2, HALF, KVW), BF),
            pltpu.VMEM((NSEQ, NCTX + 8, LANES), F32),
            pltpu.VMEM((NSEQ * NCTX, LANES), F32),
            pltpu.VMEM((8, LANES), F32),
            pltpu.VMEM((2, 3, 8, LANES), F32),
            pltpu.VMEM((2, 3, NSEQ * NCTX, LANES), F32),
            pltpu.VMEM((NSEQ, 2, HD, LANES), BF),
            pltpu.VMEM((3, NSEQ, 2, HD, LANES), BF),
            pltpu.VMEM((NSEQ, 2, HD, LANES), BF),
            pltpu.VMEM((3, NSEQ, 2, HD, LANES), BF),
            pltpu.VMEM((NSEQ, 2, HD, LANES), F32),
            pltpu.VMEM((NSEQ, 2, LEN, LANES), BF),
            pltpu.VMEM((NSEQ, 2, LEN, LANES), BF),
            pltpu.VMEM((2 * QBS, ROWS, LANES), F32),
            pltpu.VMEM((NSEQ, LEN, WIDTH), F32),
            pltpu.VMEM((2, SLOTS * BLK, LANES), BF),
            pltpu.VMEM((2, SLOTS * BLK, LANES), BF),
            pltpu.VMEM((2 * QBS * ROWS, LANES), BF),
            pltpu.VMEM((2, ROWS, LANES), BF),
            pltpu.VMEM((2, ROWS, SLOTS * BLK), F32),
            pltpu.VMEM((2, ROWS, SLOTS * BLK), BF),
            pltpu.VMEM((2, ROWS, LANES), F32),
            pltpu.VMEM((16, LANES), F32),
            pltpu.VMEM((NHEAD - 1, 16, LANES), F32),
            pltpu.VMEM((NSEQ * QBS, BLK, WIDTH), BF),
            dma((NSEQ * QBS,)),
            dma,
            dma((NSEQ, 2, 10)),
            dma((NSEQ, 2, 10)),
            dma((6,)),
            dma((6,)),
            dma((2, 4)),
            dma((2, 4)),
            dma((NHEAD - 1,)),
            dma((NHEAD - 1,)),
        ],
        compiler_params=pltpu.CompilerParams(
            vmem_limit_bytes=60 << 20, collective_id=0, has_side_effects=True
        ),
    )(
        starts,
        block_lists,
        queries,
        keys_values.reshape(NSEQ, QBS, 2, HALF, KVW),
        norm_gain,
    )


def solution(mesh):
    return jax.shard_map(
        on_device,
        mesh=mesh,
        in_specs=(
            P(None, "ctx", "head"),
            P(None, "ctx", "head"),
            P(None, "ctx", None),
            P(),
            P("head"),
        ),
        out_specs=P(None, "ctx", "head"),
        check_vma=False,
    )
```

```python
import math

import jax
import jax.numpy as jnp
from jax import lax
from jax.experimental import pallas as pl
from jax.experimental.pallas import tpu as pltpu
from jax.sharding import PartitionSpec as P

HD = 96
BLK = 128
QBS = 3
TOPK = 16
NSEQ = 4
SIDE = 4
NCTX = 16
NHEAD = 8
GROUP = 4
LANES = 128
LEN = QBS * BLK
KVW = 4 * HD
WIDTH = 2 * GROUP * HD
ROWS = GROUP * BLK
HALF = BLK // 2
OWN0 = NCTX - 1
SLOTS = OWN0 + QBS
NCH = SLOTS // 2
TAIL = LANES - HD
epsilon = 1e-06
NEG = -1e30
SCALE = math.log2(math.e) / math.sqrt(HD)
NT = (((1,), (1,)), ((), ()))
TN = (((0,), (0,)), ((), ()))
NN = (((1,), (0,)), ((), ()))
BF = jnp.bfloat16
F32 = jnp.float32
MESH = pl.DeviceIdType.MESH


def dot(a, b, dims):
    return lax.dot_general(a, b, dims, preferred_element_type=F32)


def feature(x):
    x = x.astype(F32)
    return jnp.where(x > 0, x + 1.0, jnp.exp(jnp.minimum(x, 0.0)))


def kernel(
    starts, lists, q_hbm, kv, gain, out_hbm,
    q_ref, near, packed, far, relay, bias_ref, pickrows, pickpack, pk_raw, pk_in, st_own, st_y, st_row, st_x,
    prior, fk, vown, lin_ref, comb, kx, vx, qx, fq, sc, pw, mx, sq, sq_in,
    out_ref, out_sem, q_sem, s_send, s_recv, p_send, p_recv, t_send, t_recv, h_send, h_recv,
):
    me = lax.axis_index("ctx")
    hd = lax.axis_index("head")
    x, y = me // SIDE, me % SIDE

    def device(o, du, dv):
        dx, dy = (du, dv) if o == 0 else (dv, du)
        return ((x + dx + 2 * SIDE) % SIDE) * SIDE + (y + dy + 2 * SIDE) % SIDE

    def copy(src, dst, send, recv, target):
        return pltpu.make_async_remote_copy(
            src_ref=src, dst_ref=dst, send_sem=send, recv_sem=recv,
            device_id={"ctx": target}, device_id_type=MESH,
        )

    q_copy = pltpu.make_async_copy(q_hbm, q_ref, q_sem)
    q_copy.start()
    barrier = pltpu.get_barrier_semaphore()
    for o in range(2):
        for d in range(1, SIDE):
            pl.semaphore_signal(
                barrier, inc=1, device_id={"ctx": device(o, d, 0)}, device_id_type=MESH
            )
    for d in range(1, NHEAD):
        pl.semaphore_signal(
            barrier, inc=1, device_id={"head": (hd + d) % NHEAD}, device_id_type=MESH
        )
    pl.semaphore_wait(barrier, 2 * (SIDE - 1) + NHEAD - 1)

    def pick_copy(o, d):
        i = o * 3 + d - 1
        return copy(pickpack, pk_raw.at[o, d - 1], p_send.at[i], p_recv.at[i], device(o, 0, -d))

    def hop(b, h, i):
        part = HALF // 2
        src, dst, du, dv = [
            (kv.at[b, :, h], near.at[b, h, 0], 1, 0),
            (kv.at[b, :, h], near.at[b, h, 2], -1, 0),
            (near.at[b, h, 0, :, 0:part], near.at[b, h, 1, :, 0:part], 1, 0),
            (near.at[b, h, 2, :, part:HALF], near.at[b, h, 1, :, part:HALF], -1, 0),
            (packed.at[b, h, 0], far.at[b, h, 0], 0, 1),
            (packed.at[b, h, 2], far.at[b, h, 2], 0, -1),
            (packed.at[b, h, 1, 0:2], relay.at[b, h, 0], 0, 1),
            (packed.at[b, h, 1, 2:4], relay.at[b, h, 1], 0, -1),
            (relay.at[b, h, 0], far.at[b, h, 1, 0:2], 0, 1),
            (relay.at[b, h, 1], far.at[b, h, 1, 2:4], 0, -1),
        ][i]
        return copy(src, dst, s_send.at[b, h, i], s_recv.at[b, h, i], device(h, du, dv))

    def start(b, *which):
        for i in which:
            for h in range(2):
                hop(b, h, i).start()

    def arrived(b, *which):
        for i in which:
            for h in range(2):
                hop(b, h, i).wait_recv()

    start(0, 0, 1)
    start(1, 0, 1)

    lane16 = lax.broadcasted_iota(jnp.int32, (NCTX, LANES), 1)
    lane8 = lax.broadcasted_iota(jnp.int32, (8, LANES), 1)
    match = lane16 == lax.broadcasted_iota(jnp.int32, (NCTX, LANES), 0)
    pickpack[...] = jnp.zeros((8, LANES), F32)
    sq[...] = jnp.zeros((16, LANES), F32)
    of3 = lax.broadcasted_iota(jnp.int32, (NCTX, TOPK), 0) * QBS
    mine = lax.broadcasted_iota(jnp.int32, (8, TOPK), 0) + me * QBS
    for b in range(NSEQ):
        pick = jnp.zeros((NCTX, 1), F32)
        away = jnp.zeros((NCTX, LANES), F32)
        home = jnp.zeros((8, LANES), F32)
        for qb in range(QBS):
            entry = lists[b, qb : qb + 1, :]
            off = jnp.broadcast_to(entry, (NCTX, TOPK)) - of3
            hit = (off >= 0) & (off < QBS)
            named = jnp.max(jnp.where(hit, 1.0, 0.0), axis=1, keepdims=True)
            pick = jnp.maximum(
                pick, jnp.max(jnp.where(hit, off, 0).astype(F32), axis=1, keepdims=True)
            )
            away = jnp.where((lane16 == HD + qb) & (named < 0.5), NEG, away)
            held = jnp.broadcast_to(entry, (8, TOPK)) == mine
            named = jnp.max(jnp.where(held, 1.0, 0.0), axis=1, keepdims=True)
            home = jnp.where((lane8 == HD + qb) & (named < 0.5), NEG, home)
        bias_ref[b, 0:NCTX] = away
        bias_ref[b, NCTX : NCTX + 8] = home
        spread = jnp.broadcast_to(pick, (NCTX, LANES))
        pickrows[b * NCTX : (b + 1) * NCTX] = spread
        pickpack[b : b + 1, :] = jnp.sum(jnp.where(match, spread, 0.0), axis=0, keepdims=True)
    for o in range(2):
        for d in range(1, SIDE):
            pick_copy(o, d).start()

    row96 = lax.broadcasted_iota(jnp.int32, (BLK, HD), 0)
    lane = lax.broadcasted_iota(jnp.int32, (BLK, TAIL), 1)
    row = lax.broadcasted_iota(jnp.int32, (BLK, TAIL), 0)
    zeros = jnp.zeros((BLK, TAIL), BF)
    ones = jnp.ones((BLK, TAIL), BF)

    def own_block(b, k, left, right):
        return jnp.concatenate([kv[b, k, 0, :, left:right], kv[b, k, 1, :, left:right]], axis=0)

    def summary(b, carry):
        first = starts[b]
        for k in range(QBS):
            at = slice(k * BLK, (k + 1) * BLK)
            live = row96 + (me * QBS + k) * BLK >= first
            for g in range(2):
                key = own_block(b, k, 2 * g * HD, (2 * g + 1) * HD)
                f = jnp.where(live, feature(key), 0.0).astype(BF)
                fk[b, g, at, :] = jnp.concatenate([f, zeros], axis=1)
                v = own_block(b, k, (2 * g + 1) * HD, (2 * g + 2) * HD)
                vown[b, g, at, :] = jnp.concatenate([v, ones], axis=1)
        for g in range(2):
            t = dot(fk[b, g], vown[b, g], TN)
            st_own[b, g] = t[:HD].astype(BF)
        return carry

    lax.fori_loop(0, NSEQ, summary, 0)

    def state_copy(o, i):
        own, got = (st_row, st_x) if o == 0 else (st_own, st_y)
        part = NSEQ // 2
        src, dst, du = [
            (own, got.at[0], 1),
            (own, got.at[2], -1),
            (got.at[0, 0:part], got.at[1, 0:part], 1),
            (got.at[2, part:NSEQ], got.at[1, part:NSEQ], -1),
        ][i]
        return copy(src, dst, t_send.at[o, i], t_recv.at[o, i], device(o, du, 0))

    def pass_on(b):
        arrived(b, 0, 1)
        start(b, 2, 3)

    def relay_on(b):
        arrived(b, 6, 7)
        start(b, 8, 9)

    def source(o, du, dv):
        return device(o, -du, -dv)

    def choose(table, at, blocks):
        w = jnp.broadcast_to(table[pl.ds(at, 1), :], (HALF, LANES)).astype(BF)
        m0, m1 = w == 0.0, w == 1.0
        out = []
        for c in range(KVW // LANES):
            b0, b1, b2 = [blocks[k, :, c * LANES : (c + 1) * LANES] for k in range(QBS)]
            out.append(jnp.where(m0, b0, jnp.where(m1, b1, b2)))
        return jnp.concatenate(out, axis=1)

    def pack(b):
        arrived(b, 2, 3)
        for h in range(2):
            for dv in range(1, SIDE):
                for du in range(SIDE):
                    blocks = kv.at[b, :, h] if du == 0 else near.at[b, h, du - 1]
                    packed[b, h, dv - 1, du] = choose(
                        pk_in.at[h, dv - 1], b * NCTX + source(h, du, 0), blocks
                    )
        start(b, 6, 7, 4, 5)

    for i in (0, 1):
        state_copy(1, i).start()
    pass_on(0)
    pass_on(1)
    for i in (0, 1):
        state_copy(1, i).wait_recv()
    for i in (2, 3):
        state_copy(1, i).start()
    for o in range(2):
        for d in range(1, SIDE):
            pick_copy(o, d).wait_recv()
            for b in range(NSEQ):
                line = jnp.broadcast_to(pk_raw[o, d - 1, b : b + 1, :], (NCTX, LANES))
                col = jnp.sum(jnp.where(match, line, 0.0), axis=1, keepdims=True)
                pk_in[o, d - 1, b * NCTX : (b + 1) * NCTX] = jnp.broadcast_to(col, (NCTX, LANES))
    pack(0)
    for i in (2, 3):
        state_copy(1, i).wait_recv()

    def rows_sum(b, carry):
        for g in range(2):
            total = st_own[b, g].astype(F32)
            before = jnp.zeros((HD, LANES), F32)
            for d in range(1, SIDE):
                part = st_y[d - 1, b, g].astype(F32)
                total = total + part
                before = before + jnp.where(y >= d, part, 0.0)
            st_row[b, g] = total.astype(BF)
            prior[b, g] = before
        return carry

    lax.fori_loop(0, NSEQ, rows_sum, 0)
    for i in (0, 1):
        state_copy(0, i).start()
    start(2, 0, 1)
    pack(1)
    start(3, 0, 1)
    relay_on(0)
    for i in (0, 1):
        state_copy(0, i).wait_recv()
    for i in (2, 3):
        state_copy(0, i).start()
    pass_on(2)
    q_copy.wait()
    for i in (2, 3):
        state_copy(0, i).wait_recv()

    def add_x(b, carry):
        for g in range(2):
            before = prior[b, g]
            for d in range(1, SIDE):
                before = before + jnp.where(x >= d, st_x[d - 1, b, g].astype(F32), 0.0)
            prior[b, g] = before
        return carry

    lax.fori_loop(0, NSEQ, add_x, 0)

    trow = lax.broadcasted_iota(jnp.int32, (ROWS, BLK), 0) % BLK
    tlane = lax.broadcasted_iota(jnp.int32, (ROWS, BLK), 1)
    causal = trow >= tlane

    def live_rows(b, qb):
        r = lax.broadcasted_iota(jnp.int32, (ROWS, 1), 0) % BLK
        return r + (me * QBS + qb) * BLK >= starts[b]

    def linear(b):
        for g in range(2):
            state = jnp.concatenate([prior[b, g], jnp.zeros((TAIL, LANES), F32)], axis=0)
            for qb in range(QBS):
                marks = jnp.where((lane == qb) | (lane == QBS), 1.0, 0.0).astype(BF)
                base = (g * QBS + qb) * ROWS
                for h in range(GROUP):
                    c = (g * GROUP + h) * HD
                    piece = q_ref[b, qb * BLK : (qb + 1) * BLK, c : c + HD]
                    fq[qb % 2, h * BLK : (h + 1) * BLK, :] = jnp.concatenate(
                        [feature(piece).astype(BF), zeros], axis=1
                    )
                    qx[base + h * BLK : base + (h + 1) * BLK, :] = jnp.concatenate(
                        [piece, marks], axis=1
                    )
                fqv = fq[qb % 2]
                fkv = fk[b, g, qb * BLK : (qb + 1) * BLK, :]
                vo = vown[b, g, qb * BLK : (qb + 1) * BLK, :]
                inner = jnp.where(causal, dot(fqv, fkv, NT), 0.0).astype(BF)
                high = state.astype(BF)
                low = (state - high.astype(F32)).astype(BF)
                lin = dot(inner, vo, NN) + dot(fqv, high, NN) + dot(fqv, low, NN)
                if qb < QBS - 1:
                    state = state + dot(fkv, vo, TN)
                den = jnp.where(live_rows(b, qb), lin[:, HD : HD + 1], 1.0)
                lin_ref[g * QBS + qb] = lin * (1.0 / den)

    def place(first, count, load, bias):
        at = slice(first, first + count)
        for g in range(2):
            k = load(2 * g * HD, (2 * g + 1) * HD)
            v = load((2 * g + 1) * HD, (2 * g + 2) * HD)
            kx[g, at, :] = jnp.concatenate([k, bias], axis=1)
            vx[g, at, :] = jnp.concatenate([v, ones[:count]], axis=1)

    def tail_bias(b, slot_row, pos):
        listed = bias_ref[b, pl.ds(slot_row, 1), HD:LANES]
        late = jnp.where((lane == QBS) & (row.astype(F32) + pos < starts[b].astype(F32)), NEG, 0.0)
        return (listed + late).astype(BF)

    def scores(i):
        g, qb = i // QBS, i % QBS
        q = qx[i * ROWS : (i + 1) * ROWS, :]
        top = None
        for c in range(NCH):
            at = slice(c * 2 * BLK, (c + 1) * 2 * BLK)
            s = dot(q, kx[g, at, :], NT)
            parts = []
            for n in range(2):
                k = 2 * c + n - OWN0
                part = s[:, n * BLK : (n + 1) * BLK]
                if k == qb:
                    part = jnp.where(causal, part, NEG)
                parts.append(part)
                sc[i % 2, :, (2 * c + n) * BLK : (2 * c + n + 1) * BLK] = part
            t = jnp.maximum(parts[0], parts[1])
            top = t if top is None else jnp.maximum(top, t)
        mx[i % 2] = top

    def weigh(b, i):
        g, qb = i // QBS, i % QBS
        peak = jnp.max(mx[i % 2], axis=1, keepdims=True)
        for c in range(NCH):
            at = slice(c * 2 * BLK, (c + 1) * 2 * BLK)
            pw[i % 2, :, at] = jnp.exp2((sc[i % 2, :, at] - peak) * SCALE).astype(BF)
        acc = dot(pw[i % 2], vx[g], NN)
        both = lin_ref[i] + acc * (1.0 / acc[:, HD : HD + 1])
        both = jnp.where(live_rows(b, qb), both, 0.0)
        comb[b, qb * BLK : (qb + 1) * BLK, g * GROUP * HD : (g + 1) * GROUP * HD] = (
            jnp.concatenate([both[h * BLK : (h + 1) * BLK, :HD] for h in range(GROUP)], axis=1)
        )

    def attend(b, carry):
        linear(b)
        arrived(b, 4, 5, 8, 9)
        for c in range(NSEQ - 1):

            @pl.when(b == c)
            def _(c=c):
                relay_on(c + 1)
                if c + 2 < NSEQ:
                    pack(c + 2)
                if c == 0:
                    pass_on(3)

        slot = 0
        for dx in range(SIDE):
            for dy in range(SIDE):
                if dx == 0 and dy == 0:
                    continue
                s = source(0, dx, dy)
                at = b * NCTX + s
                pos = (pickrows[pl.ds(at, 1), HD:LANES] + (s * QBS).astype(F32)) * BLK
                tb = tail_bias(b, s, pos)
                for h in range(2):
                    du, dv = (dx, dy) if h == 0 else (dy, dx)
                    if dv == 0:
                        whole = choose(pickrows, at, near.at[b, h, du - 1])
                    else:
                        whole = far[b, h, dv - 1, du]
                    place(
                        slot * BLK + h * HALF, HALF, lambda l, r, w=whole: w[:, l:r],
                        tb[h * HALF : (h + 1) * HALF],
                    )
                slot += 1
        for k in range(QBS):
            pos = ((me * QBS + k) * BLK).astype(F32)
            tb = tail_bias(b, NCTX + k, pos)
            place(slot * BLK, BLK, lambda l, r, k=k: own_block(b, k, l, r), tb)
            slot += 1
        scores(0)
        for i in range(2 * QBS):
            if i + 1 < 2 * QBS:
                scores(i + 1)
            weigh(b, i)
        for qb in range(QBS):
            c = comb[b, qb * BLK : (qb + 1) * BLK, :]
            c2 = c * c
            high = c2.astype(BF)
            low = (c2 - high.astype(F32)).astype(BF)
            e = jnp.ones((8, WIDTH), BF)
            sq[pl.ds(b * QBS + qb, 1), :] = (dot(e, high, NT) + dot(e, low, NT))[0:1]
        return carry

    lax.fori_loop(0, NSEQ, attend, 0)

    def sq_copy(d):
        return pltpu.make_async_remote_copy(
            src_ref=sq, dst_ref=sq_in.at[d - 1], send_sem=h_send.at[d - 1],
            recv_sem=h_recv.at[d - 1], device_id={"head": (hd + d) % NHEAD}, device_id_type=MESH,
        )

    for d in range(1, NHEAD):
        sq_copy(d).start()
    for d in range(1, NHEAD):
        sq_copy(d).wait_recv()

    eye = lax.broadcasted_iota(jnp.int32, (BLK, BLK), 0) == lax.broadcasted_iota(
        jnp.int32, (BLK, BLK), 1
    )
    scale_by = gain[...].astype(F32).reshape(1, WIDTH)

    def out_copy(n):
        rows = pl.ds(pl.multiple_of(n % QBS * BLK, BLK), BLK) if not isinstance(n, int) else pl.ds(n % QBS * BLK, BLK)
        return pltpu.make_async_copy(out_ref.at[n], out_hbm.at[n // QBS, rows], out_sem.at[n])

    def finish(n, carry):
        total = sq[pl.ds(n, 1), :]
        for d in range(1, NHEAD):
            total = total + sq_in[d - 1, pl.ds(n, 1), :]
        r = lax.rsqrt(total / (WIDTH * NHEAD) + epsilon)
        col = jnp.sum(jnp.where(eye, jnp.broadcast_to(r, (BLK, BLK)), 0.0), axis=1, keepdims=True)
        b, qb = n // QBS, n % QBS
        at = pl.ds(pl.multiple_of(qb * BLK, BLK), BLK)
        out_ref[n] = (comb[b, at, :] * col * scale_by).astype(BF)
        out_copy(n).start()
        return carry

    lax.fori_loop(0, NSEQ * QBS, finish, 0)
    for n in range(NSEQ * QBS):
        out_copy(n).wait()

    for d in range(1, NHEAD):
        sq_copy(d).wait_send()
    for o in range(2):
        for d in range(1, SIDE):
            pick_copy(o, d).wait_send()
        for i in range(4):
            state_copy(o, i).wait_send()
    for b in range(NSEQ):
        for h in range(2):
            for i in range(10):
                hop(b, h, i).wait_send()


def on_device(queries, keys_values, block_lists, starts, norm_gain):
    smem = pl.BlockSpec(memory_space=pltpu.SMEM)
    vmem = pl.BlockSpec(memory_space=pltpu.VMEM)
    dma = pltpu.SemaphoreType.DMA
    return pl.pallas_call(
        kernel,
        in_specs=[smem, vmem, pl.BlockSpec(memory_space=pl.ANY), vmem, vmem],
        out_specs=pl.BlockSpec(memory_space=pl.ANY),
        out_shape=jax.ShapeDtypeStruct((NSEQ, LEN, WIDTH), BF),
        scratch_shapes=[
            pltpu.VMEM((NSEQ, LEN, WIDTH), BF),
            pltpu.VMEM((NSEQ, 2, 3, QBS, HALF, KVW), BF),
            pltpu.VMEM((NSEQ, 2, 3, SIDE, HALF, KVW), BF),
            pltpu.VMEM((NSEQ, 2, 3, SIDE, HALF, KVW), BF),
            pltpu.VMEM((NSEQ, 2, 2, 2, HALF, KVW), BF),
            pltpu.VMEM((NSEQ, NCTX + 8, LANES), F32),
            pltpu.VMEM((NSEQ * NCTX, LANES), F32),
            pltpu.VMEM((8, LANES), F32),
            pltpu.VMEM((2, 3, 8, LANES), F32),
            pltpu.VMEM((2, 3, NSEQ * NCTX, LANES), F32),
            pltpu.VMEM((NSEQ, 2, HD, LANES), BF),
            pltpu.VMEM((3, NSEQ, 2, HD, LANES), BF),
            pltpu.VMEM((NSEQ, 2, HD, LANES), BF),
            pltpu.VMEM((3, NSEQ, 2, HD, LANES), BF),
            pltpu.VMEM((NSEQ, 2, HD, LANES), F32),
            pltpu.VMEM((NSEQ, 2, LEN, LANES), BF),
            pltpu.VMEM((NSEQ, 2, LEN, LANES), BF),
            pltpu.VMEM((2 * QBS, ROWS, LANES), F32),
            pltpu.VMEM((NSEQ, LEN, WIDTH), F32),
            pltpu.VMEM((2, SLOTS * BLK, LANES), BF),
            pltpu.VMEM((2, SLOTS * BLK, LANES), BF),
            pltpu.VMEM((2 * QBS * ROWS, LANES), BF),
            pltpu.VMEM((2, ROWS, LANES), BF),
            pltpu.VMEM((2, ROWS, SLOTS * BLK), F32),
            pltpu.VMEM((2, ROWS, SLOTS * BLK), BF),
            pltpu.VMEM((2, ROWS, LANES), F32),
            pltpu.VMEM((16, LANES), F32),
            pltpu.VMEM((NHEAD - 1, 16, LANES), F32),
            pltpu.VMEM((NSEQ * QBS, BLK, WIDTH), BF),
            dma((NSEQ * QBS,)),
            dma,
            dma((NSEQ, 2, 10)),
            dma((NSEQ, 2, 10)),
            dma((6,)),
            dma((6,)),
            dma((2, 4)),
            dma((2, 4)),
            dma((NHEAD - 1,)),
            dma((NHEAD - 1,)),
        ],
        compiler_params=pltpu.CompilerParams(
            vmem_limit_bytes=60 << 20, collective_id=0, has_side_effects=True
        ),
    )(
        starts,
        block_lists,
        queries,
        keys_values.reshape(NSEQ, QBS, 2, HALF, KVW),
        norm_gain,
    )


def solution(mesh):
    return jax.shard_map(
        on_device,
        mesh=mesh,
        in_specs=(
            P(None, "ctx", "head"),
            P(None, "ctx", "head"),
            P(None, "ctx", None),
            P(),
            P("head"),
        ),
        out_specs=P(None, "ctx", "head"),
        check_vma=False,
    )
```
